32 devices in a mesh: row: 4 (over z), col: 4 (over y, x), rep: 2 (over core).
Axes of the slice: x: 2, y: 2, z: 4, core: 2. Of those that a mesh axis runs over, the one named last changes fastest.
Arguments:
- features: bfloat16 [4096, 512], P(('row', 'col', 'rep')), may hold values from -6 to 6
- w_self: bfloat16 [512, 512], replicated, may hold values from -0.25 to 0.25
- w_neigh: bfloat16 [512, 512], replicated, may hold values from -1.0546875 to 1.0546875
- cotangent: bfloat16 [4096, 512], P(('row', 'col', 'rep')), may hold values from -6 to 6
- tile_row: int32 [2560], P(('row', 'col', 'rep')), may hold values from 0 to 7
- tile_col: int32 [2560], P(('row', 'col', 'rep')), may hold values from 0 to 7
- tile_mask: int32 [2560, 128, 128], P(('row', 'col', 'rep')), may hold values from 0 to 1
- tile_count: int32 [32], P(('row', 'col', 'rep')), may hold values from 20 to 80, as said below
Outputs:
- activated: bfloat16 [4096, 512], P(('row', 'col', 'rep'))
- grad_features: bfloat16 [4096, 512], P(('row', 'col', 'rep'))
- grad_weights: float32 [1024, 512], P(('row', 'col', 'rep'))
The draws below stay inside these ranges and needn't reach their ends.
Inputs may be any that keep to these rules, and one draw needn't show every extreme that they name: `tile_count`: slots below a device's count hold its live tiles; the others are ignored. Some device's count is 80.
All inputs are finite; a program needn't handle non-finite values.
Results may differ from the reference program's by a relative error of at most 0.0055.
Values may be sent and summed in bfloat16 or wider, within the bound.
A program may use at most 128 MiB of HBM per device.

```python
import math
import jax
import jax.numpy as jnp
from jax import lax

D = 512
TILE = 128
SLOTS = 80
ROW_BLOCKS = 8
COL_BLOCKS = 8
NDEV = 32
NODES = 4096
N_ROW = 4
N_COL = 4
N_REP = 2


def draw_tile_count(key, part):
    first_key, second_key = jax.random.split(key)
    total_devices = N_ROW * N_COL * N_REP
    counts = jax.random.randint(first_key, (total_devices,), SLOTS // 4, SLOTS + 1, dtype=jnp.int32)
    chosen = jax.random.randint(second_key, (), 0, total_devices, dtype=jnp.int32)
    return jnp.where(jnp.arange(total_devices, dtype=jnp.int32) == chosen, SLOTS, counts).astype(jnp.int32)


def draw_tile_mask(key, part):
    first_key, second_key = jax.random.split(key)
    total_slots = N_ROW * N_COL * N_REP * SLOTS
    groups = N_COL * N_REP
    slot_group = jnp.arange(total_slots, dtype=jnp.int32) // SLOTS % groups
    density = 2 + 4 * slot_group // max(groups - 1, 1)
    row_factor = jax.random.randint(first_key, (total_slots, TILE, 1), 1, 4, dtype=jnp.int32)
    raw_values = jax.random.randint(second_key, (total_slots, TILE, TILE), 0, 8 * TILE, dtype=jnp.int32)
    return (raw_values < density[:, None, None] * row_factor).astype(jnp.int32)


def plant(entries, key, low, top_value):
    extent = entries.shape
    index_at = [jax.random.randint(jax.random.fold_in(key, axis), (), 0, extent[axis]) for axis in range(len(extent))]
    entries = entries.at[tuple(index_at)].set(low)
    longest = extent.index(max(extent))
    index_at[longest] = (index_at[longest] + 1) % extent[longest]
    return entries.at[tuple(index_at)].set(top_value)


def level_of(stream_key, shape, shards, low, top_value):
    def one(dim, blocks):
        draws = jax.random.uniform(jax.random.fold_in(jax.random.fold_in(stream_key, 6), dim), (blocks,), jnp.float32, low / len(shards), top_value / len(shards))
        return jnp.repeat(jnp.exp(draws), shape[dim] // blocks).reshape((-1,) + (1,) * (len(shape) - dim - 1))

    level = one(*shards[0])
    for cut in shards[1:]:
        level = level * one(*cut)
    return level


def scatter_about(rng, extent, width, bound, pieces=(), held_as=jnp.bfloat16):
    drawn = jax.random.normal(rng, extent, jnp.float32) * width
    if len(pieces) > 0:
        drawn = level_of(rng, extent, pieces, -0.22, 0.18) * drawn
    return jnp.clip(drawn, min=-bound, max=bound).astype(held_as)


def setup_inputs(seed: int = 0) -> dict:
    streams_of = jax.random.split(jax.random.key(seed), 9)
    features = scatter_about(streams_of[0], (NODES, D), 1.0, 6.0, ((0, 32),))
    w_self = scatter_about(streams_of[1], (D, D), D ** -0.5, 0.25)
    w_neigh = scatter_about(streams_of[2], (D, D), (4 * D ** -0.5), 1.0546875)
    cotangent = scatter_about(streams_of[3], (NODES, D), 1.0, 6.0, ((0, 32),))
    tile_row = plant(jax.random.randint(streams_of[4], (NDEV * SLOTS,), 0, ROW_BLOCKS), jax.random.fold_in(streams_of[4], 1), 0, ROW_BLOCKS - 1).astype(jnp.int32)
    tile_col = plant(jax.random.randint(streams_of[5], (NDEV * SLOTS,), 0, COL_BLOCKS), jax.random.fold_in(streams_of[5], 1), 0, COL_BLOCKS - 1).astype(jnp.int32)
    tile_mask = draw_tile_mask(jax.random.fold_in(streams_of[8], 71), 0)
    tile_count = draw_tile_count(jax.random.fold_in(streams_of[8], 71), 0)
    return dict(features=features, w_self=w_self, w_neigh=w_neigh, cotangent=cotangent, tile_row=tile_row, tile_col=tile_col, tile_mask=tile_mask, tile_count=tile_count)


HIGHEST_PRECISION = lax.Precision.HIGHEST

def device_tiles(device, tile_row, tile_col, tile_mask, tile_count):
    slot_ids = jnp.arange(SLOTS, dtype=jnp.int32)
    first_slot = (device * SLOTS).astype(jnp.int32)
    row_ids = lax.dynamic_slice_in_dim(tile_row, first_slot, SLOTS)
    col_ids = lax.dynamic_slice_in_dim(tile_col, first_slot, SLOTS)
    tile_masks = lax.dynamic_slice_in_dim(tile_mask, first_slot, SLOTS, 0)
    live_slots = (slot_ids < tile_count[device]).astype(jnp.float32)
    tile_weights = tile_masks.astype(jnp.float32) * live_slots[:, None, None]
    row_owner = device // ROW_BLOCKS
    col_owner = device // N_REP % N_COL
    dest_blocks = (row_owner * ROW_BLOCKS + row_ids).astype(jnp.int32)
    source_blocks = (col_ids // N_REP * ROW_BLOCKS + col_owner * N_REP + col_ids % N_REP).astype(jnp.int32)
    return (dest_blocks, source_blocks, tile_weights)

def reference(features, w_self, w_neigh, cotangent, tile_row, tile_col, tile_mask, tile_count):
    feature_blocks = features.reshape(NDEV, TILE, D).astype(jnp.float32)
    device_ids = jnp.arange(NDEV, dtype=jnp.int32)

    def gather_step(carry, device):
        totals, degree = carry
        dest_blocks, source_blocks, tile_weights = device_tiles(device, tile_row, tile_col, tile_mask, tile_count)
        product = jnp.einsum('tij,tjd->tid', tile_weights, feature_blocks[source_blocks], precision=HIGHEST_PRECISION)
        totals = totals.at[dest_blocks].add(product)
        degree = degree.at[dest_blocks].add(lax.optimization_barrier(jnp.sum(tile_weights, axis=2)))
        return ((totals, degree), None)
    initial = (jnp.zeros((NDEV, TILE, D), jnp.float32), jnp.zeros((NDEV, TILE), jnp.float32))
    (totals, degree), unused = lax.scan(gather_step, initial, device_ids)
    divisor = degree.reshape(NODES, 1) + 1.0
    aggregate = (totals.reshape(NODES, D) / divisor).astype(jnp.bfloat16)
    preact = jnp.dot(features, w_self, preferred_element_type=jnp.float32) + jnp.dot(aggregate, w_neigh, preferred_element_type=jnp.float32)
    activated, pullback = jax.vjp(lambda value: jax.nn.gelu(value, approximate=True), preact)
    pre_grad = pullback(cotangent.astype(jnp.float32))[0].astype(jnp.bfloat16)
    inv_root = 1.0 / math.sqrt(NODES)
    grad_weights = jnp.concatenate([jnp.dot(features.T, pre_grad, preferred_element_type=jnp.float32), jnp.dot(aggregate.T, pre_grad, preferred_element_type=jnp.float32)], axis=0) * inv_root
    neighbour_grad = (jnp.dot(pre_grad, w_neigh.T, preferred_element_type=jnp.float32) / divisor).astype(jnp.bfloat16)
    grad_blocks = neighbour_grad.reshape(NDEV, TILE, D).astype(jnp.float32)

    def spread_step(spread, device):
        dest_blocks, source_blocks, tile_weights = device_tiles(device, tile_row, tile_col, tile_mask, tile_count)
        product = jnp.einsum('tij,tid->tjd', tile_weights, grad_blocks[dest_blocks], precision=HIGHEST_PRECISION)
        return (spread.at[source_blocks].add(product), None)
    spread, unused = lax.scan(spread_step, jnp.zeros((NDEV, TILE, D), jnp.float32), device_ids)
    grad_features = (jnp.dot(pre_grad, w_self.T, preferred_element_type=jnp.float32) + spread.reshape(NODES, D)).astype(jnp.bfloat16)
    return (activated.astype(jnp.bfloat16), grad_features, grad_weights)
```

```python
import math

import jax
import jax.numpy as jnp
from jax import lax
from jax.experimental import pallas as pl
from jax.experimental.pallas import tpu as pltpu
from jax.sharding import PartitionSpec as P

MESH_ID = pl.DeviceIdType.MESH
F32 = jnp.float32
BF16 = jnp.bfloat16
ROOT = math.sqrt(2.0 / math.pi)


def build_kernel(group, tile, rows_ref, cols_ref, count_ref, mask_ref, adj_ref):
    step = pl.program_id(0)

    @pl.when(step == 0)
    def _():
        adj_ref[...] = jnp.zeros_like(adj_ref)

    for lane in range(group):
        slot = step * group + lane

        @pl.when(slot < count_ref[0])
        def _():
            row = pl.multiple_of(rows_ref[slot] * tile, tile)
            col = pl.multiple_of(cols_ref[slot] * tile, tile)
            where = (pl.ds(row, tile), pl.ds(col, tile))
            adj_ref[where] += mask_ref[lane].astype(jnp.float32).astype(jnp.bfloat16)


def build_adjacency(tile_row, tile_col, tile_count, tile_mask, row_blocks, col_blocks):
    slots, tile, _ = tile_mask.shape
    group = math.gcd(slots, 8)
    shape = (row_blocks * tile, col_blocks * tile)
    return pl.pallas_call(
        lambda *refs: build_kernel(group, tile, *refs),
        out_shape=jax.ShapeDtypeStruct(shape, jnp.bfloat16),
        grid_spec=pltpu.PrefetchScalarGridSpec(
            num_scalar_prefetch=3,
            grid=(slots // group,),
            in_specs=[pl.BlockSpec((group, tile, tile), lambda step, *_: (step, 0, 0))],
            out_specs=pl.BlockSpec(shape, lambda step, *_: (0, 0)),
        ),
        compiler_params=pltpu.CompilerParams(vmem_limit_bytes=48 * 2**20),
        cost_estimate=pl.CostEstimate(
            flops=slots * tile * tile, bytes_accessed=slots * tile * tile * 4, transcendentals=0
        ),
    )(tile_row, tile_col, tile_count, tile_mask)


def dot(a, b, dims=((1,), (0,))):
    return lax.dot_general(a, b, (dims, ((), ())), preferred_element_type=F32)


def layer_kernel(
    rows, tile, depth,
    adj_ref, feat_ref, wself_ref, wneigh_ref, cot_ref,
    act_ref, gfeat_ref, gw_ref,
    own_adj, row_in, col_in, row_adj, col_adj, nodes, total_out, total_in,
    deg_in, rdeg, feat_t, agg_t, lhs, pgs, spread_out, spread_in, gw_out, gw_in,
    local_sem, send_sem, recv_sem,
):
    r, c, p = lax.axis_index("row"), lax.axis_index("col"), lax.axis_index("rep")
    other = 1 - p
    me = c * 2 + p
    mine = r * 2 + p
    span = 2 * tile

    def column(k):
        return (c // 2 + k // 2) % 2 * 2 + (c % 2 + k % 2) % 2

    used = [0]

    def send(src, dst, device):
        at = used[0]
        used[0] += 1
        copy = pltpu.make_async_remote_copy(
            src_ref=src, dst_ref=dst, send_sem=send_sem.at[at], recv_sem=recv_sem.at[at],
            device_id=device, device_id_type=MESH_ID,
        )
        copy.start()
        return copy

    sibling = (r, c, other)
    line = [((r + k) % rows, c, p) for k in range(1, rows)]
    plane = [(r, column(k), p) for k in range(1, 4)]
    plane_all = plane + [(r, column(k), other) for k in range(4)]

    load = pltpu.make_async_copy(adj_ref, own_adj, local_sem.at[0])
    load.start()
    barrier = pltpu.get_barrier_semaphore()
    for peer in line + plane_all:
        pl.semaphore_signal(barrier, inc=1, device_id=peer, device_id_type=MESH_ID)
    pl.semaphore_wait(barrier, rows - 1 + 7)

    copies = []
    line_copies = [send(feat_ref, nodes.at[mine], peer) for peer in line]
    copies.append(send(feat_ref, nodes.at[mine], sibling))
    sib_feat = [copies[-1]]
    adj_rows = send(adj_ref.at[:, other], row_in, sibling)
    adj_cols = [
        send(adj_ref.at[:, :, :, pl.ds(pl.multiple_of((k * 2 + other) * tile, tile), tile)],
             col_in.at[k], sibling)
        for k in range(rows)
    ]
    nodes[mine] = feat_ref[...]

    load.wait()
    ones = jnp.ones((8, rows * span), BF16)
    sums = dot(ones, own_adj[...].reshape(8 * tile, rows * span), ((1,), (1,)))
    which = lax.broadcasted_iota(jnp.int32, (8, tile), 0)
    packed = jnp.zeros((8, tile), F32)
    for k in range(8):
        packed += jnp.where(which == k, sums[:, k * tile : (k + 1) * tile], 0.0)
    deg_in[0] = packed
    deg_copies = [send(deg_in.at[0], deg_in.at[k + 1], peer) for k, peer in enumerate(plane_all)]

    feat = feat_ref[...]
    feat_t[...] = feat.astype(F32).T.astype(BF16).reshape(feat_t.shape)
    lhs[me, pl.ds(0, 2)] = feat_t[:, me]
    ft_copies = [
        send(feat_t.at[:, peer[1] * 2 + peer[2]], lhs.at[me, pl.ds(0, 2)], peer)
        for peer in plane_all
    ]
    own_part = dot(feat, wself_ref[...])

    adj_rows.wait_recv()
    row_adj[...] = own_adj[:, p].reshape(4, tile, rows * span) + row_in[...]

    for k in range(1, rows):
        line_copies[k - 1].wait_recv()
        block = (r + rows - k) % rows * 2 + p
        sib_feat.append(send(nodes.at[block], nodes.at[block], sibling))

    for copy in deg_copies:
        copy.wait_recv()
    degree = deg_in[0]
    for k in range(1, 8):
        degree += deg_in[k]
    reciprocal = 1.0 / (degree + 1.0)
    rdeg[...] = reciprocal
    scale = jnp.concatenate([reciprocal[k : k + 1] for k in range(8)], axis=1)
    for k in range(rows):
        adj_cols[k].wait_recv()
        at = pl.multiple_of((k * 2 + p) * tile, tile)
        own = own_adj[:, :, :, pl.ds(at, tile)].reshape(8 * tile, tile).astype(F32)
        both = own + col_in[k].reshape(8 * tile, tile).astype(F32)
        col_adj[pl.ds(k * tile, tile), :] = (both.T * scale).astype(BF16)

    for copy in sib_feat:
        copy.wait_recv()
    total = dot(
        row_adj[...].reshape(4 * tile, rows * span), nodes[...].reshape(rows * span, depth)
    )
    total_out[...] = total.astype(BF16).reshape(4, tile, depth)
    total_copies = [
        send(total_out.at[column(k)], total_in.at[k - 1], plane[k - 1]) for k in range(1, 4)
    ]
    mean_sum = total_out[c].astype(F32)
    for k in range(1, 4):
        total_copies[k - 1].wait_recv()
        mean_sum += total_in[k - 1].astype(F32)
    divide = jnp.broadcast_to(rdeg[pl.ds(me, 1), :], (8, tile)).T[:, 0:1]
    aggregate = (mean_sum * divide).astype(BF16)
    value = own_part + dot(aggregate, wneigh_ref[...])
    inner = jnp.tanh(ROOT * (value + 0.044715 * value * value * value))
    act_ref[...] = (0.5 * value * (1.0 + inner)).astype(BF16)
    slope = 0.5 * (1.0 + inner) + 0.5 * value * (1.0 - inner * inner) * (
        ROOT * (1.0 + 3.0 * 0.044715 * value * value)
    )
    pre_grad = (cot_ref[...].astype(F32) * slope).astype(BF16)
    pgs[me] = pre_grad
    pg_copies = [send(pgs.at[me], pgs.at[me], peer) for peer in plane]
    sib_pg = [send(pgs.at[me], pgs.at[me], sibling)]
    agg_t[...] = aggregate.astype(F32).T.astype(BF16).reshape(agg_t.shape)
    lhs[me, pl.ds(2, 2)] = agg_t[:, me]
    at_copies = [
        send(agg_t.at[:, peer[1] * 2 + peer[2]], lhs.at[me, pl.ds(2, 2)], peer)
        for peer in plane_all
    ]
    self_grad = dot(pre_grad, wself_ref[...], ((1,), (1,)))

    for k in range(1, 4):
        pg_copies[k - 1].wait_recv()
        block = column(k) * 2 + p
        sib_pg.append(send(pgs.at[block], pgs.at[block], sibling))
    for copy in sib_pg:
        copy.wait_recv()
    grads = pgs[...].reshape(8 * tile, depth)
    spread = dot(col_adj[...], grads)
    spread_out[...] = spread.astype(BF16).reshape(rows, tile, depth)
    spread_copies = [
        send(spread_out.at[(r + k) % rows], spread_in.at[k - 1], line[k - 1])
        for k in range(1, rows)
    ]

    for copy in ft_copies + at_copies:
        copy.wait_recv()
    part = jnp.zeros((4 * feat_t.shape[2], depth), F32)
    for k in range(8):
        part += dot(lhs[k].reshape(tile, tile), pgs[k])
    gw_out[...] = part.astype(BF16).reshape(gw_out.shape)
    gw_copies = [
        send(gw_out.at[(r + k) % rows], gw_in.at[k - 1], line[k - 1]) for k in range(1, rows)
    ]
    back = spread_out[r].astype(F32)
    for k in range(1, rows):
        spread_copies[k - 1].wait_recv()
        back += spread_in[k - 1].astype(F32)
    gfeat_ref[...] = (
        self_grad + dot(back.astype(BF16), wneigh_ref[...], ((1,), (1,)))
    ).astype(BF16)
    grad = gw_out[r].astype(F32)
    for k in range(1, rows):
        gw_copies[k - 1].wait_recv()
        grad += gw_in[k - 1].astype(F32)
    gw_ref[...] = grad * (1.0 / math.sqrt(tile * rows * 8))

    for copy in (
        line_copies + sib_feat + [adj_rows] + adj_cols + deg_copies + ft_copies + total_copies
        + pg_copies + sib_pg + at_copies + spread_copies + gw_copies
    ):
        copy.wait_send()


def fused_layer(adjacency, features, w_self, w_neigh, cotangent, rows):
    tile, depth = features.shape
    piece = depth // 16
    nsem = (rows - 1) + rows + 1 + rows + 7 + 7 + 3 + 3 + 4 + 7 + 2 * (rows - 1)
    width = rows * 2 * tile
    vmem = pl.BlockSpec(memory_space=pltpu.VMEM)
    return pl.pallas_call(
        lambda *refs: layer_kernel(rows, tile, depth, *refs),
        out_shape=(
            jax.ShapeDtypeStruct((tile, depth), BF16),
            jax.ShapeDtypeStruct((tile, depth), BF16),
            jax.ShapeDtypeStruct((piece, depth), F32),
        ),
        in_specs=[pl.BlockSpec(memory_space=pl.ANY)] + [vmem] * 4,
        out_specs=(vmem, vmem, vmem),
        scratch_shapes=[
            pltpu.VMEM((4, 2, tile, width), BF16),
            pltpu.VMEM((4, tile, width), BF16),
            pltpu.VMEM((rows, 4, 2, tile, tile), BF16),
            pltpu.VMEM((4, tile, width), BF16),
            pltpu.VMEM((rows * tile, 8 * tile), BF16),
            pltpu.VMEM((rows * 2, tile, depth), BF16),
            pltpu.VMEM((4, tile, depth), BF16),
            pltpu.VMEM((3, tile, depth), BF16),
            pltpu.VMEM((8, 8, tile), F32),
            pltpu.VMEM((8, tile), F32),
            pltpu.VMEM((2, 8, piece, tile), BF16),
            pltpu.VMEM((2, 8, piece, tile), BF16),
            pltpu.VMEM((8, 4, piece, tile), BF16),
            pltpu.VMEM((8, tile, depth), BF16),
            pltpu.VMEM((rows, tile, depth), BF16),
            pltpu.VMEM((rows - 1, tile, depth), BF16),
            pltpu.VMEM((rows, piece, depth), BF16),
            pltpu.VMEM((rows - 1, piece, depth), BF16),
            pltpu.SemaphoreType.DMA((1,)),
            pltpu.SemaphoreType.DMA((nsem,)),
            pltpu.SemaphoreType.DMA((nsem,)),
        ],
        compiler_params=pltpu.CompilerParams(
            collective_id=0, has_side_effects=True, vmem_limit_bytes=48 * 2**20
        ),
        name="layer",
    )(adjacency.reshape(4, 2, tile, width), features, w_self, w_neigh, cotangent)


def shards(features, w_self, w_neigh, cotangent, tile_row, tile_col, tile_mask, tile_count):
    row_devices = lax.axis_size("row")
    col_devices = lax.axis_size("col")
    rep_devices = lax.axis_size("rep")
    device_total = row_devices * col_devices * rep_devices
    tile_size = features.shape[0]
    row_blocks = col_devices * rep_devices
    col_blocks = row_devices * rep_devices
    adjacency = build_adjacency(tile_row, tile_col, tile_count, tile_mask, row_blocks, col_blocks)
    if (row_devices, col_devices, rep_devices) == (4, 4, 2):
        return fused_layer(adjacency, features, w_self, w_neigh, cotangent, row_devices)
    gathered = lax.all_gather(features, ("row", "rep"), axis=0, tiled=True)
    totals = jnp.dot(adjacency, gathered, preferred_element_type=jnp.float32)
    degree = jnp.sum(adjacency.astype(jnp.float32), axis=1)
    own_sum, own_degree = (
        lax.psum_scatter(totals, ("col", "rep"), scatter_dimension=0, tiled=True),
        lax.psum_scatter(degree, ("col", "rep"), scatter_dimension=0, tiled=True),
    )
    divisor = own_degree[:, None] + 1.0
    aggregate = (own_sum / divisor).astype(jnp.bfloat16)
    preact = jnp.dot(features, w_self, preferred_element_type=jnp.float32) + jnp.dot(
        aggregate, w_neigh, preferred_element_type=jnp.float32
    )
    activated, pullback = jax.vjp(lambda value: jax.nn.gelu(value, approximate=True), preact)
    pre_grad = pullback(cotangent.astype(jnp.float32))[0].astype(jnp.bfloat16)
    inv_root = 1.0 / math.sqrt(tile_size * device_total)
    local_grads = (
        jnp.concatenate(
            [
                jnp.dot(features.T, pre_grad, preferred_element_type=jnp.float32),
                jnp.dot(aggregate.T, pre_grad, preferred_element_type=jnp.float32),
            ],
            axis=0,
        )
        * inv_root
    )
    neighbour_grad = (
        jnp.dot(pre_grad, w_neigh.T, preferred_element_type=jnp.float32) / divisor
    ).astype(jnp.bfloat16)
    slab_grads = lax.all_gather(neighbour_grad, ("col", "rep"), axis=0, tiled=True)
    grad_weights = lax.psum_scatter(
        local_grads, ("row", "col", "rep"), scatter_dimension=0, tiled=True
    )
    spread = lax.dot_general(
        adjacency, slab_grads, (((0,), (0,)), ((), ())), preferred_element_type=jnp.float32
    )
    returned = lax.psum_scatter(spread, ("row", "rep"), scatter_dimension=0, tiled=True)
    grad_features = (
        jnp.dot(pre_grad, w_self.T, preferred_element_type=jnp.float32) + returned
    ).astype(jnp.bfloat16)
    return (activated.astype(jnp.bfloat16), grad_features, grad_weights)


def solution(mesh):
    placed = (
        P(("row", "col", "rep"), None),
        P(),
        P(),
        P(("row", "col", "rep"), None),
        P(("row", "col", "rep")),
        P(("row", "col", "rep")),
        P(("row", "col", "rep"), None, None),
        P(("row", "col", "rep")),
    )
    return jax.shard_map(
        shards,
        mesh=mesh,
        in_specs=placed,
        out_specs=(
            P(("row", "col", "rep"), None),
            P(("row", "col", "rep"), None),
            P(("row", "col", "rep"), None),
        ),
        check_vma=False,
    )
```

```python
import math

import jax
import jax.numpy as jnp
from jax import lax
from jax.experimental import pallas as pl
from jax.experimental.pallas import tpu as pltpu
from jax.sharding import PartitionSpec as P

MESH_ID = pl.DeviceIdType.MESH
F32 = jnp.float32
BF16 = jnp.bfloat16
ROOT = math.sqrt(2.0 / math.pi)


def build_kernel(group, tile, rows_ref, cols_ref, count_ref, mask_ref, adj_ref):
    step = pl.program_id(0)

    @pl.when(step == 0)
    def _():
        adj_ref[...] = jnp.zeros_like(adj_ref)

    for lane in range(group):
        slot = step * group + lane

        @pl.when(slot < count_ref[0])
        def _():
            row = pl.multiple_of(rows_ref[slot] * tile, tile)
            col = pl.multiple_of(cols_ref[slot] * tile, tile)
            where = (pl.ds(row, tile), pl.ds(col, tile))
            adj_ref[where] += mask_ref[lane].astype(jnp.float32).astype(jnp.bfloat16)


def build_adjacency(tile_row, tile_col, tile_count, tile_mask, row_blocks, col_blocks):
    slots, tile, _ = tile_mask.shape
    group = math.gcd(slots, 8)
    shape = (row_blocks * tile, col_blocks * tile)
    return pl.pallas_call(
        lambda *refs: build_kernel(group, tile, *refs),
        out_shape=jax.ShapeDtypeStruct(shape, jnp.bfloat16),
        grid_spec=pltpu.PrefetchScalarGridSpec(
            num_scalar_prefetch=3,
            grid=(slots // group,),
            in_specs=[pl.BlockSpec((group, tile, tile), lambda step, *_: (step, 0, 0))],
            out_specs=pl.BlockSpec(shape, lambda step, *_: (0, 0)),
        ),
        compiler_params=pltpu.CompilerParams(vmem_limit_bytes=48 * 2**20),
        cost_estimate=pl.CostEstimate(
            flops=slots * tile * tile, bytes_accessed=slots * tile * tile * 4, transcendentals=0
        ),
    )(tile_row, tile_col, tile_count, tile_mask)


def dot(a, b, dims=((1,), (0,))):
    return lax.dot_general(a, b, (dims, ((), ())), preferred_element_type=F32)


CHUNKS = 2


def layer_kernel(
    tile, depth, slots, chunks,
    feat_ref, wself_ref, wneigh_ref, cot_ref, trow_ref, tcol_ref, count_ref, mask_ref,
    act_ref, gfeat_ref, gw_ref,
    feat, wself, wneigh, cot, trow, tcol, count, mask, place,
    own_adj, row_in, col_in, row_adj, col_adj, nodes, total_out, total_in,
    deg_in, rdeg, feat_t, agg_t, lhs, pgs, spread_out, spread_in, gw_out, gw_in,
    value, aggregate, self_grad,
    local_sem, mask_sem, send_sem, recv_sem,
):
    r, c, p = lax.axis_index("row"), lax.axis_index("col"), lax.axis_index("rep")
    other = 1 - p
    me = c * 2 + p
    mine = r * 2 + p
    wide = 8 * tile
    part = depth // chunks

    def cols(q):
        return pl.ds(q * part, part)

    low = 1 - r // 2
    middle = r * low + (3 - r) * (1 - low)

    def place_of(v):
        return low * v + (1 - low) * (3 - v)

    def at_row(v):
        return (place_of(v), c, p)

    def column(k):
        return (c // 2 + k // 2) % 2 * 2 + (c % 2 + k % 2) % 2

    used = [0]
    begun = []

    def copy_to(src, dst, device):
        at = used[0]
        used[0] += 1
        return pltpu.make_async_remote_copy(
            src_ref=src, dst_ref=dst, send_sem=send_sem.at[at], recv_sem=recv_sem.at[at],
            device_id=device, device_id_type=MESH_ID,
        )

    def send(src, dst, device):
        copy = copy_to(src, dst, device)
        copy.start()
        begun.append(copy)
        return copy


    def arrived(copy):
        copy.wait_recv()

    sibling = (r, c, other)
    line = [((r + k) % 4, c, p) for k in range(1, 4)]
    plane = [(r, column(k), p) for k in range(1, 4)]
    plane_all = plane + [(r, column(k), other) for k in range(4)]

    loads = [
        pltpu.make_async_copy(a, b, local_sem.at[i])
        for i, (a, b) in enumerate((
            (trow_ref, trow), (tcol_ref, tcol), (count_ref, count), (feat_ref, feat),
            (wself_ref, wself), (wneigh_ref, wneigh), (cot_ref, cot),
        ))
    ]
    for load in loads[:3]:
        load.start()
    groups = [
        pltpu.make_async_copy(mask_ref.at[:, pl.ds(g * 16, 16), :], mask.at[g], mask_sem.at[g])
        for g in range(tile // 16)
    ]
    for load in loads[3:4]:
        load.start()
    for group in groups:
        group.start()
    for load in loads[4:]:
        load.start()

    barrier = pltpu.get_barrier_semaphore()
    for peer in line + plane_all:
        pl.semaphore_signal(barrier, inc=1, device_id=peer, device_id_type=MESH_ID)

    for load in loads[:3]:
        load.wait()
    lane = lax.broadcasted_iota(jnp.int32, (8, slots), 1)
    cell = jnp.broadcast_to((trow[...] * 8 + tcol[...]).reshape(1, slots), (8, slots))
    cell = jnp.where(lane < count[0], cell, 64).astype(F32).astype(BF16)
    gap = lax.broadcasted_iota(jnp.int32, (slots, slots * 8), 1) - 8 * lax.broadcasted_iota(
        jnp.int32, (slots, slots * 8), 0
    )
    repeat = jnp.where((gap >= 0) & (gap < 8), 1.0, 0.0).astype(BF16)
    key = dot(cell, repeat)[0:1] * 8.0 + (
        lax.broadcasted_iota(jnp.int32, (1, slots * 8), 1) % 8
    ).astype(F32)
    spot = lax.broadcasted_iota(jnp.int32, (512, slots * 8), 0).astype(F32)
    place[...] = jnp.where(spot == key, 1.0, 0.0).astype(BF16)

    pl.semaphore_wait(barrier, 10)

    near, across, inward, outward, onward, sib_feat = [], [], [], [], [], []
    for q in range(chunks):
        src, dst = feat_ref.at[:, cols(q)], nodes.at[q, mine]
        far = nodes.at[q, place_of(3) * 2 + p]
        near.append(copy_to(src, dst, at_row(1 - middle)))
        across.append(copy_to(src, dst, at_row(2)))
        inward.append(copy_to(src, dst, at_row(2)))
        outward.append(copy_to(src, dst, at_row(3)))
        onward.append(copy_to(far, far, at_row(0)))

        @pl.when(middle == 0)
        def _():
            inward[q].start()

        @pl.when(middle == 1)
        def _():
            outward[q].start()
            across[q].start()

        near[q].start()

    for q in range(chunks):
        sib_feat.append([send(feat_ref.at[:, cols(q)], nodes.at[q, mine], sibling)])

    def build(g, carry):
        pltpu.make_async_copy(
            mask_ref.at[:, pl.ds(g * 16, 16), :], mask.at[g], mask_sem.at[g]
        ).wait()
        x = jnp.concatenate(
            [
                mask[g, :, 0:8, :].reshape(slots * 8, tile).astype(F32).astype(BF16),
                mask[g, :, 8:16, :].reshape(slots * 8, tile).astype(F32).astype(BF16),
            ],
            axis=1,
        )
        res = dot(place[...], x)
        for i in range(8):
            for j in range(8):
                at = (i * 8 + j) * 8
                both = jnp.concatenate([res[at : at + 8, :tile], res[at : at + 8, tile:]], axis=0)
                own_adj[i // 2, i % 2, pl.ds(pl.multiple_of(g * 16, 16), 16),
                        j * tile : (j + 1) * tile] = both.astype(BF16)
        return carry

    lax.fori_loop(0, tile // 16, build, 0)

    adj_rows = send(own_adj.at[:, other], row_in, sibling)
    adj_cols = [
        send(own_adj.at[:, :, :, pl.ds(pl.multiple_of((k * 2 + other) * tile, tile), tile)],
             col_in.at[k], sibling)
        for k in range(4)
    ]

    def line_arrivals(q):
        def onto(k):
            block = nodes.at[q, place_of(k) * 2 + p]
            sib_feat[q].append(send(block, block, sibling))

        near[q].wait_recv()
        onto(1 - middle)

        @pl.when(middle == 1)
        def _():
            inward[q].wait_recv()
            onward[q].start()
            across[q].wait_recv()

        @pl.when(middle == 0)
        def _():
            outward[q].wait_recv()

        onto(2)

        @pl.when(middle == 0)
        def _():
            onward[q].wait_recv()

        onto(3)

    for load in loads[3:]:
        load.wait()
    for q in range(chunks):
        nodes[q, mine] = feat[:, q * part : (q + 1) * part]

    ones = jnp.ones((8, wide), BF16)
    sums = dot(ones, own_adj[...].reshape(wide, wide), ((1,), (1,)))
    which = lax.broadcasted_iota(jnp.int32, (8, tile), 0)
    packed = jnp.zeros((8, tile), F32)
    for k in range(8):
        packed += jnp.where(which == k, sums[:, k * tile : (k + 1) * tile], 0.0)
    deg_in[0] = packed
    deg_copies = [send(deg_in.at[0], deg_in.at[k + 1], peer) for k, peer in enumerate(plane_all)]

    line_arrivals(0)
    arrived(adj_rows)
    row_adj[...] = own_adj[:, p].reshape(4, tile, wide) + row_in[...]

    total_copies = []

    def neighbour_sums(q):
        for copy in sib_feat[q]:
            arrived(copy)
        total = dot(row_adj[...].reshape(4 * tile, wide), nodes[q].reshape(wide, part))
        total_out[q] = total.astype(BF16).reshape(4, tile, part)
        total_copies.append([
            send(total_out.at[q, column(k)], total_in.at[q, k - 1], plane[k - 1])
            for k in range(1, 4)
        ])

    neighbour_sums(0)
    for q in range(1, chunks):
        line_arrivals(q)
        neighbour_sums(q)

    feat_t[...] = feat[...].astype(F32).T.astype(BF16).reshape(feat_t.shape)
    here = pl.ds(pl.multiple_of(me * tile, tile), tile)
    lhs[pl.ds(0, 2), :, here] = feat_t[:, me]
    slices = [
        send(feat_t.at[:, peer[1] * 2 + peer[2]], lhs.at[pl.ds(0, 2), :, here], peer)
        for peer in plane_all
    ]
    value[...] = dot(feat[...], wself[...])

    for copy in deg_copies:
        arrived(copy)
    degree = deg_in[0]
    for k in range(1, 8):
        degree += deg_in[k]
    reciprocal = 1.0 / (degree + 1.0)
    rdeg[...] = reciprocal
    scale = jnp.concatenate([reciprocal[k : k + 1] for k in range(8)], axis=1)
    divide = jnp.broadcast_to(rdeg[pl.ds(me, 1), :], (8, tile)).T[:, 0:1]
    for k in range(4):
        arrived(adj_cols[k])
        at = pl.multiple_of((k * 2 + p) * tile, tile)
        both = own_adj[:, :, :, pl.ds(at, tile)] + col_in[k]
        both = both.reshape(wide, tile).astype(F32)
        col_adj[pl.ds(k * tile, tile), :] = (both.T * scale).astype(BF16)

    for q in range(chunks):
        mean_sum = total_out[q, c].astype(F32)
        for k in range(1, 4):
            arrived(total_copies[q][k - 1])
            mean_sum += total_in[q, k - 1].astype(F32)
        aggregate[:, cols(q)] = (mean_sum * divide).astype(BF16)
        if q < chunks - 1:
            value[...] += dot(aggregate[:, cols(q)], wneigh[cols(q), :])
    pg_copies, sib_pg = [], []
    for q in range(chunks):
        v = value[:, cols(q)] + dot(
            aggregate[:, cols(chunks - 1)], wneigh[cols(chunks - 1), cols(q)]
        )
        inner = jnp.tanh(ROOT * (v + 0.044715 * v * v * v))
        act_ref[:, cols(q)] = (0.5 * v * (1.0 + inner)).astype(BF16)
        slope = 0.5 * (1.0 + inner) + 0.5 * v * (1.0 - inner * inner) * (
            ROOT * (1.0 + 3.0 * 0.044715 * v * v)
        )
        pgs[q, me] = (cot[:, cols(q)].astype(F32) * slope).astype(BF16)
        pg_copies.append([send(pgs.at[q, me], pgs.at[q, me], peer) for peer in plane])
        sib_pg.append([send(pgs.at[q, me], pgs.at[q, me], sibling)])
    agg_t[...] = aggregate[...].astype(F32).T.astype(BF16).reshape(agg_t.shape)
    lhs[pl.ds(2, 2), :, here] = agg_t[:, me]
    slices += [
        send(agg_t.at[:, peer[1] * 2 + peer[2]], lhs.at[pl.ds(2, 2), :, here], peer)
        for peer in plane_all
    ]
    total_self = dot(pgs[0, me], wself[:, cols(0)], ((1,), (1,)))
    for q in range(1, chunks):
        total_self += dot(pgs[q, me], wself[:, cols(q)], ((1,), (1,)))
    self_grad[...] = total_self

    relay, near_s, second_s, third_s = [], [], [], []
    for q in range(chunks):
        for k in range(1, 4):
            arrived(pg_copies[q][k - 1])
            at = column(k) * 2 + p
            sib_pg[q].append(send(pgs.at[q, at], pgs.at[q, at], sibling))
        for copy in sib_pg[q]:
            arrived(copy)
        spread = dot(col_adj[...], pgs[q].reshape(wide, part))
        spread_out[q] = spread.astype(BF16).reshape(4, tile, part)
        relay.append(copy_to(spread_out.at[q, place_of(3)], spread_in.at[q, 3], at_row(1)))
        third_s.append(copy_to(spread_out.at[q, place_of(2)], spread_in.at[q, 2], at_row(2)))
        near_s.append(
            copy_to(spread_out.at[q, place_of(1 - middle)], spread_in.at[q, 0], at_row(1 - middle))
        )
        second_s.append((
            copy_to(spread_out.at[q, place_of(2)], spread_in.at[q, 1], at_row(2)),
            copy_to(spread_out.at[q, place_of(3)], spread_in.at[q, 1], at_row(3)),
        ))

        @pl.when(middle == 0)
        def _():
            relay[q].start()
            third_s[q].start()

        @pl.when(middle == 1)
        def _():
            second_s[q][0].start()

        near_s[q].start()

    for copy in slices:
        arrived(copy)
    for q in range(chunks):
        gw_out[:, :, cols(q)] = (
            dot(lhs[...].reshape(tile, wide), pgs[q].reshape(wide, part))
            .astype(BF16)
            .reshape(4, tile // 4, part)
        )

    @pl.when(middle == 1)
    def _():
        for q in range(chunks):
            relay[q].wait_recv()
            joint = spread_out[q, place_of(3)].astype(F32) + spread_in[q, 3].astype(F32)
            spread_out[q, place_of(3)] = joint.astype(BF16)
            second_s[q][1].start()

    gw_copies = [
        send(gw_out.at[(r + k) % 4], gw_in.at[k - 1], line[k - 1]) for k in range(1, 4)
    ]
    total_self = self_grad[...]
    for q in range(chunks):
        near_s[q].wait_recv()
        value[:, cols(q)] = spread_out[q, r].astype(F32) + spread_in[q, 0].astype(F32)

        @pl.when(middle == 1)
        def _():
            second_s[q][0].wait_recv()
            third_s[q].wait_recv()
            value[:, cols(q)] += spread_in[q, 2].astype(F32)

        @pl.when(middle == 0)
        def _():
            second_s[q][1].wait_recv()

        back = (value[:, cols(q)] + spread_in[q, 1].astype(F32)).astype(BF16)
        total_self += dot(back, wneigh[:, cols(q)], ((1,), (1,)))
    gfeat_ref[...] = total_self.astype(BF16)
    grad = gw_out[r].astype(F32)
    for k in range(1, 4):
        gw_copies[k - 1].wait_recv()
        grad += gw_in[k - 1].astype(F32)
    gw_ref[...] = grad * (1.0 / math.sqrt(tile * 32))

    assert used[0] == send_sem.shape[0]
    for copy in begun + near + near_s:
        copy.wait_send()

    @pl.when(middle == 1)
    def _():
        for q in range(chunks):
            for copy in (across[q], outward[q], onward[q]) + second_s[q]:
                copy.wait_send()

    @pl.when(middle == 0)
    def _():
        for copy in inward + relay + third_s:
            copy.wait_send()


def fused_layer(features, w_self, w_neigh, cotangent, tile_row, tile_col, tile_mask, tile_count):
    tile, depth = features.shape
    slots = tile_mask.shape[0]
    q, part = CHUNKS, depth // CHUNKS
    piece = depth // 16
    wide = 8 * tile
    nsem = q * (5 + 4 + 3 + 3 + 4 + 5) + 5 + 7 + 14 + 3
    vmem = pl.BlockSpec(memory_space=pltpu.VMEM)
    return pl.pallas_call(
        lambda *refs: layer_kernel(tile, depth, slots, q, *refs),
        out_shape=(
            jax.ShapeDtypeStruct((tile, depth), BF16),
            jax.ShapeDtypeStruct((tile, depth), BF16),
            jax.ShapeDtypeStruct((piece, depth), F32),
        ),
        in_specs=[pl.BlockSpec(memory_space=pl.ANY)] * 8,
        out_specs=(vmem, vmem, vmem),
        scratch_shapes=[
            pltpu.VMEM((tile, depth), BF16),
            pltpu.VMEM((depth, depth), BF16),
            pltpu.VMEM((depth, depth), BF16),
            pltpu.VMEM((tile, depth), BF16),
            pltpu.VMEM((slots,), jnp.int32),
            pltpu.VMEM((slots,), jnp.int32),
            pltpu.SMEM((1,), jnp.int32),
            pltpu.VMEM((tile // 16, slots, 16, tile), jnp.int32),
            pltpu.VMEM((512, slots * 8), BF16),
            pltpu.VMEM((4, 2, tile, wide), BF16),
            pltpu.VMEM((4, tile, wide), BF16),
            pltpu.VMEM((4, 4, 2, tile, tile), BF16),
            pltpu.VMEM((4, tile, wide), BF16),
            pltpu.VMEM((4 * tile, wide), BF16),
            pltpu.VMEM((q, 8, tile, part), BF16),
            pltpu.VMEM((q, 4, tile, part), BF16),
            pltpu.VMEM((q, 3, tile, part), BF16),
            pltpu.VMEM((8, 8, tile), F32),
            pltpu.VMEM((8, tile), F32),
            pltpu.VMEM((2, 8, piece, tile), BF16),
            pltpu.VMEM((2, 8, piece, tile), BF16),
            pltpu.VMEM((4, piece, wide), BF16),
            pltpu.VMEM((q, 8, tile, part), BF16),
            pltpu.VMEM((q, 4, tile, part), BF16),
            pltpu.VMEM((q, 4, tile, part), BF16),
            pltpu.VMEM((4, piece, depth), BF16),
            pltpu.VMEM((3, piece, depth), BF16),
            pltpu.VMEM((tile, depth), F32),
            pltpu.VMEM((tile, depth), BF16),
            pltpu.VMEM((tile, depth), F32),
            pltpu.SemaphoreType.DMA((7,)),
            pltpu.SemaphoreType.DMA((tile // 16,)),
            pltpu.SemaphoreType.DMA((nsem,)),
            pltpu.SemaphoreType.DMA((nsem,)),
        ],
        compiler_params=pltpu.CompilerParams(
            collective_id=0, has_side_effects=True, vmem_limit_bytes=56 * 2**20
        ),
        name="layer",
    )(features, w_self, w_neigh, cotangent, tile_row, tile_col, tile_count, tile_mask)


def shards(features, w_self, w_neigh, cotangent, tile_row, tile_col, tile_mask, tile_count):
    row_devices = lax.axis_size("row")
    col_devices = lax.axis_size("col")
    rep_devices = lax.axis_size("rep")
    device_total = row_devices * col_devices * rep_devices
    tile_size = features.shape[0]
    row_blocks = col_devices * rep_devices
    col_blocks = row_devices * rep_devices
    if (row_devices, col_devices, rep_devices) == (4, 4, 2):
        return fused_layer(
            features, w_self, w_neigh, cotangent, tile_row, tile_col, tile_mask, tile_count
        )
    adjacency = build_adjacency(tile_row, tile_col, tile_count, tile_mask, row_blocks, col_blocks)
    gathered = lax.all_gather(features, ("row", "rep"), axis=0, tiled=True)
    totals = jnp.dot(adjacency, gathered, preferred_element_type=jnp.float32)
    degree = jnp.sum(adjacency.astype(jnp.float32), axis=1)
    own_sum, own_degree = (
        lax.psum_scatter(totals, ("col", "rep"), scatter_dimension=0, tiled=True),
        lax.psum_scatter(degree, ("col", "rep"), scatter_dimension=0, tiled=True),
    )
    divisor = own_degree[:, None] + 1.0
    aggregate = (own_sum / divisor).astype(jnp.bfloat16)
    preact = jnp.dot(features, w_self, preferred_element_type=jnp.float32) + jnp.dot(
        aggregate, w_neigh, preferred_element_type=jnp.float32
    )
    activated, pullback = jax.vjp(lambda value: jax.nn.gelu(value, approximate=True), preact)
    pre_grad = pullback(cotangent.astype(jnp.float32))[0].astype(jnp.bfloat16)
    inv_root = 1.0 / math.sqrt(tile_size * device_total)
    local_grads = (
        jnp.concatenate(
            [
                jnp.dot(features.T, pre_grad, preferred_element_type=jnp.float32),
                jnp.dot(aggregate.T, pre_grad, preferred_element_type=jnp.float32),
            ],
            axis=0,
        )
        * inv_root
    )
    neighbour_grad = (
        jnp.dot(pre_grad, w_neigh.T, preferred_element_type=jnp.float32) / divisor
    ).astype(jnp.bfloat16)
    slab_grads = lax.all_gather(neighbour_grad, ("col", "rep"), axis=0, tiled=True)
    grad_weights = lax.psum_scatter(
        local_grads, ("row", "col", "rep"), scatter_dimension=0, tiled=True
    )
    spread = lax.dot_general(
        adjacency, slab_grads, (((0,), (0,)), ((), ())), preferred_element_type=jnp.float32
    )
    returned = lax.psum_scatter(spread, ("row", "rep"), scatter_dimension=0, tiled=True)
    grad_features = (
        jnp.dot(pre_grad, w_self.T, preferred_element_type=jnp.float32) + returned
    ).astype(jnp.bfloat16)
    return (activated.astype(jnp.bfloat16), grad_features, grad_weights)


def solution(mesh):
    placed = (
        P(("row", "col", "rep"), None),
        P(),
        P(),
        P(("row", "col", "rep"), None),
        P(("row", "col", "rep")),
        P(("row", "col", "rep")),
        P(("row", "col", "rep"), None, None),
        P(("row", "col", "rep")),
    )
    return jax.shard_map(
        shards,
        mesh=mesh,
        in_specs=placed,
        out_specs=(
            P(("row", "col", "rep"), None),
            P(("row", "col", "rep"), None),
            P(("row", "col", "rep"), None),
        ),
        check_vma=False,
    )
```

```python
import math

import jax
import jax.numpy as jnp
from jax import lax
from jax.experimental import pallas as pl
from jax.experimental.pallas import tpu as pltpu
from jax.sharding import PartitionSpec as P

MESH_ID = pl.DeviceIdType.MESH
F32 = jnp.float32
BF16 = jnp.bfloat16
ROOT = math.sqrt(2.0 / math.pi)


def build_kernel(group, tile, rows_ref, cols_ref, count_ref, mask_ref, adj_ref):
    step = pl.program_id(0)

    @pl.when(step == 0)
    def _():
        adj_ref[...] = jnp.zeros_like(adj_ref)

    for lane in range(group):
        slot = step * group + lane

        @pl.when(slot < count_ref[0])
        def _():
            row = pl.multiple_of(rows_ref[slot] * tile, tile)
            col = pl.multiple_of(cols_ref[slot] * tile, tile)
            where = (pl.ds(row, tile), pl.ds(col, tile))
            adj_ref[where] += mask_ref[lane].astype(jnp.float32).astype(jnp.bfloat16)


def build_adjacency(tile_row, tile_col, tile_count, tile_mask, row_blocks, col_blocks):
    slots, tile, _ = tile_mask.shape
    group = math.gcd(slots, 8)
    shape = (row_blocks * tile, col_blocks * tile)
    return pl.pallas_call(
        lambda *refs: build_kernel(group, tile, *refs),
        out_shape=jax.ShapeDtypeStruct(shape, jnp.bfloat16),
        grid_spec=pltpu.PrefetchScalarGridSpec(
            num_scalar_prefetch=3,
            grid=(slots // group,),
            in_specs=[pl.BlockSpec((group, tile, tile), lambda step, *_: (step, 0, 0))],
            out_specs=pl.BlockSpec(shape, lambda step, *_: (0, 0)),
        ),
        compiler_params=pltpu.CompilerParams(vmem_limit_bytes=48 * 2**20),
        cost_estimate=pl.CostEstimate(
            flops=slots * tile * tile, bytes_accessed=slots * tile * tile * 4, transcendentals=0
        ),
    )(tile_row, tile_col, tile_count, tile_mask)


def dot(a, b, dims=((1,), (0,))):
    return lax.dot_general(a, b, (dims, ((), ())), preferred_element_type=F32)


CHUNKS = 2
LIMIT = 56
AHEAD = 2
P1D = 0
P4D = 0
LATE = 1


def layer_kernel(
    tile, depth, slots, chunks, ahead,
    feat_ref, wself_ref, wneigh_ref, cot_ref, trow_ref, tcol_ref, count_ref, mask_ref,
    act_ref, gfeat_ref, gw_ref,
    feat, wself, wneigh, cot, trow, tcol, count, mask, place,
    own_adj, row_in, col_in, row_adj, col_adj, nodes, total_out, total_in,
    deg_in, rdeg, feat_t, agg_t, lhs, pgs, spread_out, spread_in, gw_out, gw_in,
    value, aggregate, self_grad,
    local_sem, mask_sem, send_sem, recv_sem,
):
    r, c, p = lax.axis_index("row"), lax.axis_index("col"), lax.axis_index("rep")
    other = 1 - p
    me = c * 2 + p
    mine = r * 2 + p
    wide = 8 * tile
    part = depth // chunks

    def cols(q):
        return pl.ds(q * part, part)

    low = 1 - r // 2
    middle = r * low + (3 - r) * (1 - low)

    def place_of(v):
        return low * v + (1 - low) * (3 - v)

    def at_row(v):
        return (place_of(v), c, p)

    def column(k):
        return (c // 2 + k // 2) % 2 * 2 + (c % 2 + k % 2) % 2

    used = [0]
    begun = []
    gone = set()

    def copy_to(src, dst, device):
        at = used[0]
        used[0] += 1
        return pltpu.make_async_remote_copy(
            src_ref=src, dst_ref=dst, send_sem=send_sem.at[at], recv_sem=recv_sem.at[at],
            device_id=device, device_id_type=MESH_ID,
        )

    def send(src, dst, device):
        copy = copy_to(src, dst, device)
        copy.start()
        begun.append(copy)
        return copy


    def arrived(copy):
        copy.wait_recv()

    sibling = (r, c, other)
    line = [((r + k) % 4, c, p) for k in range(1, 4)]
    plane = [(r, column(k), p) for k in range(1, 4)]
    plane_all = plane + [(r, column(k), other) for k in range(4)]

    loads = [
        pltpu.make_async_copy(a, b, local_sem.at[i])
        for i, (a, b) in enumerate((
            (trow_ref, trow), (tcol_ref, tcol), (count_ref, count), (feat_ref, feat),
            (wself_ref, wself), (wneigh_ref, wneigh), (cot_ref, cot),
        ))
    ]
    for load in loads[:3]:
        load.start()
    groups = [
        pltpu.make_async_copy(mask_ref.at[:, pl.ds(g * 16, 16), :], mask.at[g], mask_sem.at[g])
        for g in range(tile // 16)
    ]
    for load in loads[3:4]:
        load.start()
    for group in groups:
        group.start()
    for load in loads[4:]:
        load.start()

    barrier = pltpu.get_barrier_semaphore()
    for peer in line + plane_all:
        pl.semaphore_signal(barrier, inc=1, device_id=peer, device_id_type=MESH_ID)

    for load in loads[:3]:
        load.wait()
    lane = lax.broadcasted_iota(jnp.int32, (8, slots), 1)
    cell = jnp.broadcast_to((trow[...] * 8 + tcol[...]).reshape(1, slots), (8, slots))
    cell = jnp.where(lane < count[0], cell, 64).astype(F32).astype(BF16)
    gap = lax.broadcasted_iota(jnp.int32, (slots, slots * 8), 1) - 8 * lax.broadcasted_iota(
        jnp.int32, (slots, slots * 8), 0
    )
    repeat = jnp.where((gap >= 0) & (gap < 8), 1.0, 0.0).astype(BF16)
    key = dot(cell, repeat)[0:1] * 8.0 + (
        lax.broadcasted_iota(jnp.int32, (1, slots * 8), 1) % 8
    ).astype(F32)
    spot = lax.broadcasted_iota(jnp.int32, (512, slots * 8), 0).astype(F32)
    place[...] = jnp.where(spot == key, 1.0, 0.0).astype(BF16)

    loads[3].wait()
    here = pl.ds(pl.multiple_of(me * tile, tile), tile)
    feat_t[...] = feat[...].astype(F32).T.astype(BF16).reshape(feat_t.shape)
    lhs[pl.ds(0, 2), :, here] = feat_t[:, me]
    for q in range(chunks):
        nodes[q, mine] = feat[:, q * part : (q + 1) * part]

    pl.semaphore_wait(barrier, 10)

    near, across, inward, outward, onward, sib_feat = [], [], [], [], [], []
    direct = []
    for q in range(chunks if P1D else 0):
        src, dst = feat_ref.at[:, cols(q)], nodes.at[q, mine]
        base = used[0]
        direct.append((base, [copy_to(src, dst, peer) for peer in line]))
    for q in range(0 if P1D else chunks):
        src, dst = feat_ref.at[:, cols(q)], nodes.at[q, mine]
        far = nodes.at[q, place_of(3) * 2 + p]
        near.append(copy_to(src, dst, at_row(1 - middle)))
        across.append(copy_to(src, dst, at_row(2)))
        inward.append(copy_to(src, dst, at_row(2)))
        outward.append(copy_to(src, dst, at_row(3)))
        onward.append(copy_to(far, far, at_row(0)))

    def line_start(q):
        if P1D:
            for k in (1, 0, 2):
                direct[q][1][k].start()
            return

        @pl.when(middle == 0)
        def _():
            inward[q].start()

        @pl.when(middle == 1)
        def _():
            outward[q].start()
            across[q].start()

        near[q].start()

    def line_sent(q):
        if P1D:
            for copy in direct[q][1]:
                copy.wait_send()
            return

        near[q].wait_send()

        @pl.when(middle == 0)
        def _():
            inward[q].wait_send()

        @pl.when(middle == 1)
        def _():
            outward[q].wait_send()
            across[q].wait_send()

    for q in range(min(ahead, chunks)):
        line_start(q)
    for q in range(chunks):
        sib_feat.append([send(feat_ref.at[:, cols(q)], nodes.at[q, mine], sibling)])
    slices = [
        send(feat_t.at[:, peer[1] * 2 + peer[2]], lhs.at[pl.ds(0, 2), :, here], peer)
        for peer in plane_all
    ]

    def build(g, carry):
        pltpu.make_async_copy(
            mask_ref.at[:, pl.ds(g * 16, 16), :], mask.at[g], mask_sem.at[g]
        ).wait()
        x = jnp.concatenate(
            [
                mask[g, :, 0:8, :].reshape(slots * 8, tile).astype(F32).astype(BF16),
                mask[g, :, 8:16, :].reshape(slots * 8, tile).astype(F32).astype(BF16),
            ],
            axis=1,
        )
        res = dot(place[...], x)
        for i in range(8):
            for j in range(8):
                at = (i * 8 + j) * 8
                both = jnp.concatenate([res[at : at + 8, :tile], res[at : at + 8, tile:]], axis=0)
                own_adj[i // 2, i % 2, pl.ds(pl.multiple_of(g * 16, 16), 16),
                        j * tile : (j + 1) * tile] = both.astype(BF16)
        return carry

    lax.fori_loop(0, tile // 16, build, 0)

    for q in range(ahead, chunks):
        line_sent(q - ahead)
        line_start(q)

    adj_rows = send(own_adj.at[:, other], row_in, sibling)
    adj_cols = [
        send(own_adj.at[:, :, :, pl.ds(pl.multiple_of((k * 2 + other) * tile, tile), tile)],
             col_in.at[k], sibling)
        for k in range(4)
    ]

    def line_arrivals(q):
        def onto(k):
            block = nodes.at[q, place_of(k) * 2 + p]
            sib_feat[q].append(send(block, block, sibling))

        if P1D:
            for v in (1 - middle, 2, 3):
                source = place_of(v)
                at = direct[q][0] + (r + 3 - source) % 4
                block = nodes.at[q, source * 2 + p]
                pltpu.make_async_remote_copy(
                    src_ref=block, dst_ref=block, send_sem=send_sem.at[at],
                    recv_sem=recv_sem.at[at], device_id=sibling, device_id_type=MESH_ID,
                ).wait_recv()
                onto(v)
            return

        near[q].wait_recv()
        onto(1 - middle)

        @pl.when(middle == 1)
        def _():
            inward[q].wait_recv()
            onward[q].start()
            across[q].wait_recv()

        @pl.when(middle == 0)
        def _():
            outward[q].wait_recv()

        onto(2)

        @pl.when(middle == 0)
        def _():
            onward[q].wait_recv()

        onto(3)

    for load in loads[4:]:
        load.wait()

    ones = jnp.ones((8, wide), BF16)
    sums = dot(ones, own_adj[...].reshape(wide, wide), ((1,), (1,)))
    which = lax.broadcasted_iota(jnp.int32, (8, tile), 0)
    packed = jnp.zeros((8, tile), F32)
    for k in range(8):
        packed += jnp.where(which == k, sums[:, k * tile : (k + 1) * tile], 0.0)
    deg_in[0] = packed
    deg_copies = [send(deg_in.at[0], deg_in.at[k + 1], peer) for k, peer in enumerate(plane_all)]

    line_arrivals(0)
    arrived(adj_rows)
    row_adj[...] = own_adj[:, p].reshape(4, tile, wide) + row_in[...]

    total_copies = []

    def neighbour_sums(q):
        for copy in sib_feat[q]:
            arrived(copy)
        total = dot(row_adj[...].reshape(4 * tile, wide), nodes[q].reshape(wide, part))
        total_out[q] = total.astype(BF16).reshape(4, tile, part)
        total_copies.append([
            send(total_out.at[q, column(k)], total_in.at[q, k - 1], plane[k - 1])
            for k in range(1, 4)
        ])

    value_columns = []

    def fill(q):
        if q == 0:
            value[...] = dot(feat[...], wself[...])
            for copy in deg_copies:
                arrived(copy)
            degree = deg_in[0]
            for k in range(1, 8):
                degree += deg_in[k]
            rdeg[...] = 1.0 / (degree + 1.0)
        if q == min(1, chunks - 1):
            reciprocal = rdeg[...]
            scale = jnp.concatenate([reciprocal[k : k + 1] for k in range(8)], axis=1)
            value_columns.append(jnp.broadcast_to(rdeg[pl.ds(me, 1), :], (8, tile)).T[:, 0:1])
            for k in range(4):
                arrived(adj_cols[k])
                at = pl.multiple_of((k * 2 + p) * tile, tile)
                both = own_adj[:, :, :, pl.ds(at, tile)] + col_in[k]
                both = both.reshape(wide, tile).astype(F32)
                col_adj[pl.ds(k * tile, tile), :] = (both.T * scale).astype(BF16)

    neighbour_sums(0)
    if not LATE: fill(0)
    for q in range(1, chunks):
        line_arrivals(q)
        neighbour_sums(q)
        if not LATE: fill(q)
    for q in range(chunks if LATE else 0):
        fill(q)
    divide = value_columns[0]

    for q in range(chunks):
        mean_sum = total_out[q, c].astype(F32)
        for k in range(1, 4):
            arrived(total_copies[q][k - 1])
            mean_sum += total_in[q, k - 1].astype(F32)
        aggregate[:, cols(q)] = (mean_sum * divide).astype(BF16)
        if q < chunks - 1:
            value[...] += dot(aggregate[:, cols(q)], wneigh[cols(q), :])
    pg_copies, sib_pg = [], []
    for q in range(chunks):
        v = value[:, cols(q)] + dot(
            aggregate[:, cols(chunks - 1)], wneigh[cols(chunks - 1), cols(q)]
        )
        inner = jnp.tanh(ROOT * (v + 0.044715 * v * v * v))
        act_ref[:, cols(q)] = (0.5 * v * (1.0 + inner)).astype(BF16)
        slope = 0.5 * (1.0 + inner) + 0.5 * v * (1.0 - inner * inner) * (
            ROOT * (1.0 + 3.0 * 0.044715 * v * v)
        )
        pgs[q, me] = (cot[:, cols(q)].astype(F32) * slope).astype(BF16)
        if q >= ahead:
            for copy in pg_copies[q - ahead]:
                copy.wait_send()
                gone.add(id(copy))
        pg_copies.append([send(pgs.at[q, me], pgs.at[q, me], peer) for peer in plane])
        sib_pg.append([send(pgs.at[q, me], pgs.at[q, me], sibling)])
    agg_t[...] = aggregate[...].astype(F32).T.astype(BF16).reshape(agg_t.shape)
    lhs[pl.ds(2, 2), :, here] = agg_t[:, me]
    slices += [
        send(agg_t.at[:, peer[1] * 2 + peer[2]], lhs.at[pl.ds(2, 2), :, here], peer)
        for peer in plane_all
    ]
    total_self = dot(pgs[0, me], wself[:, cols(0)], ((1,), (1,)))
    for q in range(1, chunks):
        total_self += dot(pgs[q, me], wself[:, cols(q)], ((1,), (1,)))
    self_grad[...] = total_self

    relay, near_s, second_s, third_s, straight = [], [], [], [], []

    def follow(q):
        @pl.when(middle == 0)
        def _():
            third_s[q].start()
            near_s[q].start()

        @pl.when(middle == 1)
        def _():
            relay[q].wait_recv()
            joint = spread_out[q, place_of(3)].astype(F32) + spread_in[q, 3].astype(F32)
            spread_out[q, place_of(3)] = joint.astype(BF16)
            second_s[q][1].start()

    for q in range(chunks):
        for k in range(1, 4):
            arrived(pg_copies[q][k - 1])
            at = column(k) * 2 + p
            sib_pg[q].append(send(pgs.at[q, at], pgs.at[q, at], sibling))
        for copy in sib_pg[q]:
            arrived(copy)
        spread = dot(col_adj[...], pgs[q].reshape(wide, part))
        spread_out[q] = spread.astype(BF16).reshape(4, tile, part)
        if P4D:
            straight.append([
                send(spread_out.at[q, (r + k) % 4], spread_in.at[q, k - 1], line[k - 1])
                for k in (2, 1, 3)
            ])
        else:
            relay.append(copy_to(spread_out.at[q, place_of(3)], spread_in.at[q, 3], at_row(1)))
            third_s.append(copy_to(spread_out.at[q, place_of(2)], spread_in.at[q, 2], at_row(2)))
            near_s.append(
                copy_to(spread_out.at[q, place_of(1 - middle)], spread_in.at[q, 0], at_row(1 - middle))
            )
            second_s.append((
                copy_to(spread_out.at[q, place_of(2)], spread_in.at[q, 1], at_row(2)),
                copy_to(spread_out.at[q, place_of(3)], spread_in.at[q, 1], at_row(3)),
            ))

            @pl.when(middle == 0)
            def _():
                relay[q].start()

            @pl.when(middle == 1)
            def _():
                second_s[q][0].start()
                near_s[q].start()

            if q > 0:
                follow(q - 1)
    if not P4D:
        follow(chunks - 1)

    for copy in slices:
        arrived(copy)
    for q in range(chunks):
        gw_out[:, :, cols(q)] = (
            dot(lhs[...].reshape(tile, wide), pgs[q].reshape(wide, part))
            .astype(BF16)
            .reshape(4, tile // 4, part)
        )

    gw_copies = [
        send(gw_out.at[(r + k) % 4], gw_in.at[k - 1], line[k - 1]) for k in range(1, 4)
    ]
    total_self = self_grad[...]
    for q in range(chunks):
        if P4D:
            back = spread_out[q, r].astype(F32)
            for copy, k in zip(straight[q], (2, 1, 3)):
                copy.wait_recv()
                back += spread_in[q, k - 1].astype(F32)
            total_self += dot(back.astype(BF16), wneigh[:, cols(q)], ((1,), (1,)))
            continue
        near_s[q].wait_recv()
        value[:, cols(q)] = spread_out[q, r].astype(F32) + spread_in[q, 0].astype(F32)

        @pl.when(middle == 1)
        def _():
            second_s[q][0].wait_recv()
            third_s[q].wait_recv()
            value[:, cols(q)] += spread_in[q, 2].astype(F32)

        @pl.when(middle == 0)
        def _():
            second_s[q][1].wait_recv()

        back = (value[:, cols(q)] + spread_in[q, 1].astype(F32)).astype(BF16)
        total_self += dot(back, wneigh[:, cols(q)], ((1,), (1,)))
    gfeat_ref[...] = total_self.astype(BF16)
    grad = gw_out[r].astype(F32)
    for k in range(1, 4):
        gw_copies[k - 1].wait_recv()
        grad += gw_in[k - 1].astype(F32)
    gw_ref[...] = grad * (1.0 / math.sqrt(tile * 32))

    assert used[0] <= send_sem.shape[0]
    for copy in begun + near_s:
        if id(copy) not in gone:
            copy.wait_send()
    for q in range(max(chunks - ahead, 0), chunks):
        line_sent(q)

    @pl.when(middle == 1)
    def _():
        for q in range(chunks):
            for copy in (() if P1D else (onward[q],)) + (() if P4D else second_s[q]):
                copy.wait_send()

    @pl.when(middle == 0)
    def _():
        for copy in relay + third_s:
            copy.wait_send()


def finish_kernel(act_ref, gfeat_ref, gw_ref, act_out, gfeat_out, gw_out, sem):
    copies = [
        pltpu.make_async_copy(a, b, sem.at[i])
        for i, (a, b) in enumerate(((act_ref, act_out), (gfeat_ref, gfeat_out), (gw_ref, gw_out)))
    ]
    for copy in copies:
        copy.start()
    for copy in copies:
        copy.wait()


def fused_layer(features, w_self, w_neigh, cotangent, tile_row, tile_col, tile_mask, tile_count):
    tile, depth = features.shape
    slots = tile_mask.shape[0]
    q, part = CHUNKS, depth // CHUNKS
    piece = depth // 16
    wide = 8 * tile
    nsem = q * (5 + 4 + 3 + 3 + 4 + 5) + 5 + 7 + 14 + 3
    vmem = pl.BlockSpec(memory_space=pltpu.VMEM)
    results = pl.pallas_call(
        lambda *refs: layer_kernel(tile, depth, slots, q, AHEAD, *refs),
        out_shape=(
            pltpu.VMEM((tile, depth), BF16),
            pltpu.VMEM((tile, depth), BF16),
            pltpu.VMEM((piece, depth), F32),
        ),
        in_specs=[pl.BlockSpec(memory_space=pltpu.HBM)] * 8,
        out_specs=(vmem, vmem, vmem),
        scratch_shapes=[
            pltpu.VMEM((tile, depth), BF16),
            pltpu.VMEM((depth, depth), BF16),
            pltpu.VMEM((depth, depth), BF16),
            pltpu.VMEM((tile, depth), BF16),
            pltpu.VMEM((slots,), jnp.int32),
            pltpu.VMEM((slots,), jnp.int32),
            pltpu.SMEM((1,), jnp.int32),
            pltpu.VMEM((tile // 16, slots, 16, tile), jnp.int32),
            pltpu.VMEM((512, slots * 8), BF16),
            pltpu.VMEM((4, 2, tile, wide), BF16),
            pltpu.VMEM((4, tile, wide), BF16),
            pltpu.VMEM((4, 4, 2, tile, tile), BF16),
            pltpu.VMEM((4, tile, wide), BF16),
            pltpu.VMEM((4 * tile, wide), BF16),
            pltpu.VMEM((q, 8, tile, part), BF16),
            pltpu.VMEM((q, 4, tile, part), BF16),
            pltpu.VMEM((q, 3, tile, part), BF16),
            pltpu.VMEM((8, 8, tile), F32),
            pltpu.VMEM((8, tile), F32),
            pltpu.VMEM((2, 8, piece, tile), BF16),
            pltpu.VMEM((2, 8, piece, tile), BF16),
            pltpu.VMEM((4, piece, wide), BF16),
            pltpu.VMEM((q, 8, tile, part), BF16),
            pltpu.VMEM((q, 4, tile, part), BF16),
            pltpu.VMEM((q, 4, tile, part), BF16),
            pltpu.VMEM((4, piece, depth), BF16),
            pltpu.VMEM((3, piece, depth), BF16),
            pltpu.VMEM((tile, depth), F32),
            pltpu.VMEM((tile, depth), BF16),
            pltpu.VMEM((tile, depth), F32),
            pltpu.SemaphoreType.DMA((7,)),
            pltpu.SemaphoreType.DMA((tile // 16,)),
            pltpu.SemaphoreType.DMA((nsem,)),
            pltpu.SemaphoreType.DMA((nsem,)),
        ],
        compiler_params=pltpu.CompilerParams(
            collective_id=0, has_side_effects=True, vmem_limit_bytes=LIMIT * 2**20
        ),
        name="layer",
    )(features, w_self, w_neigh, cotangent, tile_row, tile_col, tile_count, tile_mask)
    return pl.pallas_call(
        finish_kernel,
        out_shape=tuple(jax.ShapeDtypeStruct(x.shape, x.dtype) for x in results),
        in_specs=[vmem] * 3,
        out_specs=(pl.BlockSpec(memory_space=pl.ANY),) * 3,
        scratch_shapes=[pltpu.SemaphoreType.DMA((3,))],
        compiler_params=pltpu.CompilerParams(vmem_limit_bytes=2**20),
        name="finish",
    )(*results)


def shards(features, w_self, w_neigh, cotangent, tile_row, tile_col, tile_mask, tile_count):
    row_devices = lax.axis_size("row")
    col_devices = lax.axis_size("col")
    rep_devices = lax.axis_size("rep")
    device_total = row_devices * col_devices * rep_devices
    tile_size = features.shape[0]
    row_blocks = col_devices * rep_devices
    col_blocks = row_devices * rep_devices
    if (row_devices, col_devices, rep_devices) == (4, 4, 2):
        return fused_layer(
            features, w_self, w_neigh, cotangent, tile_row, tile_col, tile_mask, tile_count
        )
    adjacency = build_adjacency(tile_row, tile_col, tile_count, tile_mask, row_blocks, col_blocks)
    gathered = lax.all_gather(features, ("row", "rep"), axis=0, tiled=True)
    totals = jnp.dot(adjacency, gathered, preferred_element_type=jnp.float32)
    degree = jnp.sum(adjacency.astype(jnp.float32), axis=1)
    own_sum, own_degree = (
        lax.psum_scatter(totals, ("col", "rep"), scatter_dimension=0, tiled=True),
        lax.psum_scatter(degree, ("col", "rep"), scatter_dimension=0, tiled=True),
    )
    divisor = own_degree[:, None] + 1.0
    aggregate = (own_sum / divisor).astype(jnp.bfloat16)
    preact = jnp.dot(features, w_self, preferred_element_type=jnp.float32) + jnp.dot(
        aggregate, w_neigh, preferred_element_type=jnp.float32
    )
    activated, pullback = jax.vjp(lambda value: jax.nn.gelu(value, approximate=True), preact)
    pre_grad = pullback(cotangent.astype(jnp.float32))[0].astype(jnp.bfloat16)
    inv_root = 1.0 / math.sqrt(tile_size * device_total)
    local_grads = (
        jnp.concatenate(
            [
                jnp.dot(features.T, pre_grad, preferred_element_type=jnp.float32),
                jnp.dot(aggregate.T, pre_grad, preferred_element_type=jnp.float32),
            ],
            axis=0,
        )
        * inv_root
    )
    neighbour_grad = (
        jnp.dot(pre_grad, w_neigh.T, preferred_element_type=jnp.float32) / divisor
    ).astype(jnp.bfloat16)
    slab_grads = lax.all_gather(neighbour_grad, ("col", "rep"), axis=0, tiled=True)
    grad_weights = lax.psum_scatter(
        local_grads, ("row", "col", "rep"), scatter_dimension=0, tiled=True
    )
    spread = lax.dot_general(
        adjacency, slab_grads, (((0,), (0,)), ((), ())), preferred_element_type=jnp.float32
    )
    returned = lax.psum_scatter(spread, ("row", "rep"), scatter_dimension=0, tiled=True)
    grad_features = (
        jnp.dot(pre_grad, w_self.T, preferred_element_type=jnp.float32) + returned
    ).astype(jnp.bfloat16)
    return (activated.astype(jnp.bfloat16), grad_features, grad_weights)


def solution(mesh):
    placed = (
        P(("row", "col", "rep"), None),
        P(),
        P(),
        P(("row", "col", "rep"), None),
        P(("row", "col", "rep")),
        P(("row", "col", "rep")),
        P(("row", "col", "rep"), None, None),
        P(("row", "col", "rep")),
    )
    return jax.shard_map(
        shards,
        mesh=mesh,
        in_specs=placed,
        out_specs=(
            P(("row", "col", "rep"), None),
            P(("row", "col", "rep"), None),
            P(("row", "col", "rep"), None),
        ),
        check_vma=False,
    )
```

```python
import math

import jax
import jax.numpy as jnp
from jax import lax
from jax.experimental import pallas as pl
from jax.experimental.pallas import tpu as pltpu
from jax.sharding import PartitionSpec as P

MESH_ID = pl.DeviceIdType.MESH
F32 = jnp.float32
BF16 = jnp.bfloat16
ROOT = math.sqrt(2.0 / math.pi)


def build_kernel(group, tile, rows_ref, cols_ref, count_ref, mask_ref, adj_ref):
    step = pl.program_id(0)

    @pl.when(step == 0)
    def _():
        adj_ref[...] = jnp.zeros_like(adj_ref)

    for lane in range(group):
        slot = step * group + lane

        @pl.when(slot < count_ref[0])
        def _():
            row = pl.multiple_of(rows_ref[slot] * tile, tile)
            col = pl.multiple_of(cols_ref[slot] * tile, tile)
            where = (pl.ds(row, tile), pl.ds(col, tile))
            adj_ref[where] += mask_ref[lane].astype(jnp.float32).astype(jnp.bfloat16)


def build_adjacency(tile_row, tile_col, tile_count, tile_mask, row_blocks, col_blocks):
    slots, tile, _ = tile_mask.shape
    group = math.gcd(slots, 8)
    shape = (row_blocks * tile, col_blocks * tile)
    return pl.pallas_call(
        lambda *refs: build_kernel(group, tile, *refs),
        out_shape=jax.ShapeDtypeStruct(shape, jnp.bfloat16),
        grid_spec=pltpu.PrefetchScalarGridSpec(
            num_scalar_prefetch=3,
            grid=(slots // group,),
            in_specs=[pl.BlockSpec((group, tile, tile), lambda step, *_: (step, 0, 0))],
            out_specs=pl.BlockSpec(shape, lambda step, *_: (0, 0)),
        ),
        compiler_params=pltpu.CompilerParams(vmem_limit_bytes=48 * 2**20),
        cost_estimate=pl.CostEstimate(
            flops=slots * tile * tile, bytes_accessed=slots * tile * tile * 4, transcendentals=0
        ),
    )(tile_row, tile_col, tile_count, tile_mask)


def dot(a, b, dims=((1,), (0,))):
    return lax.dot_general(a, b, (dims, ((), ())), preferred_element_type=F32)


CHUNKS = 2
MOVE = 0
GWE = 1
FWD = 0
SIBF = 1
LIMIT = 56
AHEAD = 2
P1D = 0
P4D = 0
LATE = 1


def layer_kernel(
    tile, depth, slots, chunks, ahead,
    feat_ref, wself_ref, wneigh_ref, cot_ref, trow_ref, tcol_ref, count_ref, mask_ref,
    act_ref, gfeat_ref, gw_ref,
    feat, wself, wneigh, cot, trow, tcol, count, mask, place,
    own_adj, adj_in, row_adj, col_adj, nodes, total_out, total_in,
    deg_in, rdeg, feat_t, agg_t, lhs, pgs, spread_out, spread_in, gw_out, gw_in,
    value, aggregate, self_grad,
    local_sem, mask_sem, send_sem, recv_sem,
):
    r, c, p = lax.axis_index("row"), lax.axis_index("col"), lax.axis_index("rep")
    other = 1 - p
    me = c * 2 + p
    order = p * 4 + c
    wide, half = 8 * tile, 4 * tile
    part = depth // chunks

    def cols(q):
        return pl.ds(q * part, part)

    low = 1 - r // 2
    middle = r * low + (3 - r) * (1 - low)

    def place_of(v):
        return low * v + (1 - low) * (3 - v)

    def at_row(v):
        return (place_of(v), c, p)

    def column(k):
        return (c // 2 + k // 2) % 2 * 2 + (c % 2 + k % 2) % 2

    used = [0]
    begun = []
    gone = set()

    def copy_to(src, dst, device):
        at = used[0]
        used[0] += 1
        return pltpu.make_async_remote_copy(
            src_ref=src, dst_ref=dst, send_sem=send_sem.at[at], recv_sem=recv_sem.at[at],
            device_id=device, device_id_type=MESH_ID,
        )

    def send(src, dst, device):
        copy = copy_to(src, dst, device)
        copy.start()
        begun.append(copy)
        return copy


    def arrived(copy):
        copy.wait_recv()

    sibling = (r, c, other)
    line = [((r + k) % 4, c, p) for k in range(1, 4)]
    plane = [(r, column(k), p) for k in range(1, 4)]
    plane_all = plane + [(r, column(k), other) for k in range(4)]

    barrier = pltpu.get_barrier_semaphore()
    for peer in line + plane_all:
        pl.semaphore_signal(barrier, inc=1, device_id=peer, device_id_type=MESH_ID)

    loads = [
        pltpu.make_async_copy(a, b, local_sem.at[i])
        for i, (a, b) in enumerate((
            (trow_ref, trow), (tcol_ref, tcol), (count_ref, count), (feat_ref, feat),
            (wself_ref, wself), (wneigh_ref, wneigh), (cot_ref, cot),
        ))
    ]
    for load in loads[:3]:
        load.start()
    groups = [
        pltpu.make_async_copy(mask_ref.at[:, pl.ds(g * 16, 16), :], mask.at[g], mask_sem.at[g])
        for g in range(tile // 16)
    ]
    for load in loads[3:4]:
        load.start()
    for group in groups:
        group.start()
    for load in loads[4:]:
        load.start()

    pl.semaphore_wait(barrier, 10)

    near, across, inward, outward, onward, sib_feat = [], [], [], [], [], []
    direct = []
    for q in range(chunks if P1D else 0):
        src, dst = feat_ref.at[:, cols(q)], nodes.at[q, p, r]
        base = used[0]
        direct.append((base, [copy_to(src, dst, peer) for peer in line]))
    for q in range(0 if P1D else chunks):
        src, dst = feat_ref.at[:, cols(q)], nodes.at[q, p, r]
        far = nodes.at[q, p, place_of(3)]
        near.append(copy_to(src, dst, at_row(1 - middle)))
        across.append(copy_to(src, dst, at_row(2)))
        inward.append(copy_to(src, dst, at_row(2)))
        outward.append(copy_to(src, dst, at_row(3)))
        onward.append(copy_to(far, far, at_row(0)))

    def line_start(q):
        if P1D:
            for k in (1, 0, 2):
                direct[q][1][k].start()
            return

        @pl.when(middle == 0)
        def _():
            inward[q].start()

        @pl.when(middle == 1)
        def _():
            outward[q].start()
            across[q].start()

        near[q].start()

    def line_sent(q):
        if P1D:
            for copy in direct[q][1]:
                copy.wait_send()
            return

        near[q].wait_send()

        @pl.when(middle == 0)
        def _():
            inward[q].wait_send()

        @pl.when(middle == 1)
        def _():
            outward[q].wait_send()
            across[q].wait_send()

    if SIBF:
        for q in range(chunks):
            sib_feat.append([send(feat_ref.at[:, cols(q)], nodes.at[q, p, r], sibling)])
    for q in range(min(ahead, chunks)):
        line_start(q)
    for q in range(0 if SIBF else chunks):
        sib_feat.append([send(feat_ref.at[:, cols(q)], nodes.at[q, p, r], sibling)])
    for load in loads[:3]:
        load.wait()
    lane = lax.broadcasted_iota(jnp.int32, (8, slots), 1)
    cell = jnp.broadcast_to((trow[...] * 8 + tcol[...]).reshape(1, slots), (8, slots))
    cell = jnp.where(lane < count[0], cell, 64).astype(F32).astype(BF16)
    gap = lax.broadcasted_iota(jnp.int32, (slots, slots * 8), 1) - 8 * lax.broadcasted_iota(
        jnp.int32, (slots, slots * 8), 0
    )
    repeat = jnp.where((gap >= 0) & (gap < 8), 1.0, 0.0).astype(BF16)
    key = dot(cell, repeat)[0:1] * 8.0 + (
        lax.broadcasted_iota(jnp.int32, (1, slots * 8), 1) % 8
    ).astype(F32)
    spot = lax.broadcasted_iota(jnp.int32, (512, slots * 8), 0).astype(F32)
    place[...] = jnp.where(spot == key, 1.0, 0.0).astype(BF16)

    loads[3].wait()
    here = pl.ds(pl.multiple_of(order * tile, tile), tile)
    feat_t[...] = feat[...].astype(F32).T.astype(BF16).reshape(feat_t.shape)
    lhs[pl.ds(0, 2), :, here] = feat_t[:, me]
    for q in range(chunks):
        nodes[q, p, r] = feat[:, q * part : (q + 1) * part]
    slices = [
        send(feat_t.at[:, peer[1] * 2 + peer[2]], lhs.at[pl.ds(0, 2), :, here], peer)
        for peer in plane_all
    ]

    def build(g, carry):
        pltpu.make_async_copy(
            mask_ref.at[:, pl.ds(g * 16, 16), :], mask.at[g], mask_sem.at[g]
        ).wait()
        x = jnp.concatenate(
            [
                mask[g, :, 0:8, :].reshape(slots * 8, tile).astype(F32).astype(BF16),
                mask[g, :, 8:16, :].reshape(slots * 8, tile).astype(F32).astype(BF16),
            ],
            axis=1,
        )
        res = dot(place[...], x)
        for i in range(8):
            for j in range(8):
                at = (i * 8 + j) * 8
                both = jnp.concatenate([res[at : at + 8, :tile], res[at : at + 8, tile:]], axis=0)
                own_adj[j % 2, i % 2, i // 2, pl.ds(pl.multiple_of(g * 16, 16), 16),
                        j // 2 * tile : (j // 2 + 1) * tile] = both.astype(BF16)
        return carry

    lax.fori_loop(0, tile // 16, build, 0)

    @pl.when(middle == 1)
    def _():
        for q in range(chunks):
            inward[q].wait_recv()
            onward[q].start()

    for q in range(ahead, chunks):
        line_sent(q - ahead)
        line_start(q)

    adj_copies = [
        send(own_adj.at[b, a], adj_in.at[i], sibling)
        for i, (b, a) in enumerate(((other, other), (p, other), (other, p)))
    ]

    def line_arrivals(q):
        def onto(k):
            block = nodes.at[q, p, place_of(k)]
            sib_feat[q].append(send(block, block, sibling))

        if P1D:
            for v in (1 - middle, 2, 3):
                source = place_of(v)
                at = direct[q][0] + (r + 3 - source) % 4
                block = nodes.at[q, p, source]
                pltpu.make_async_remote_copy(
                    src_ref=block, dst_ref=block, send_sem=send_sem.at[at],
                    recv_sem=recv_sem.at[at], device_id=sibling, device_id_type=MESH_ID,
                ).wait_recv()
                onto(v)
            return

        near[q].wait_recv()
        onto(1 - middle)

        @pl.when(middle == 1)
        def _():
            across[q].wait_recv()

        @pl.when(middle == 0)
        def _():
            outward[q].wait_recv()

        onto(2)

        @pl.when(middle == 0)
        def _():
            onward[q].wait_recv()

        onto(3)

    for load in loads[4:]:
        load.wait()

    ones = jnp.ones((8, half), BF16)
    sums = dot(ones, own_adj[0].reshape(wide, half), ((1,), (1,)))
    sums += dot(ones, own_adj[1].reshape(wide, half), ((1,), (1,)))
    which = lax.broadcasted_iota(jnp.int32, (8, tile), 0)
    packed = jnp.zeros((8, tile), F32)
    for k in range(8):
        packed += jnp.where(which == k, sums[:, k * tile : (k + 1) * tile], 0.0)
    deg_in[0] = packed
    deg_copies = [send(deg_in.at[0], deg_in.at[k + 1], peer) for k, peer in enumerate(plane_all)]

    line_arrivals(0)
    arrived(adj_copies[0])
    row_adj[0] = (own_adj[p, p] + adj_in[0]).reshape(half, half)
    arrived(adj_copies[1])
    row_adj[1] = (own_adj[other, p] + adj_in[1]).reshape(half, half)

    total_copies = []

    def neighbour_sums(q):
        total = dot(row_adj[0], nodes[q, p].reshape(half, part))
        for copy in sib_feat[q]:
            arrived(copy)
        total += dot(row_adj[1], nodes[q, other].reshape(half, part))
        total_out[q] = total.astype(BF16).reshape(4, tile, part)
        total_copies.append([
            send(total_out.at[q, column(k)], total_in.at[q, k - 1], plane[k - 1])
            for k in range(1, 4)
        ])

    value_columns = []

    def fill(q):
        if q == 0:
            value[...] = dot(feat[...], wself[...])
            for copy in deg_copies:
                arrived(copy)
            degree = deg_in[0]
            for k in range(1, 8):
                degree += deg_in[k]
            rdeg[...] = 1.0 / (degree + 1.0)
        if q == min(1, chunks - 1):
            value_columns.append(jnp.broadcast_to(rdeg[pl.ds(order, 1), :], (8, tile)).T[:, 0:1])
            scales = [
                jnp.concatenate([rdeg[pl.ds(rep * 4 + k, 1), :] for k in range(4)], axis=1)
                for rep in (p, other)
            ]
            col_adj[0] = (row_adj[0].astype(F32).T * scales[0]).astype(BF16)
            arrived(adj_copies[2])
            both = (own_adj[p, other] + adj_in[2]).reshape(half, half).astype(F32)
            col_adj[1] = (both.T * scales[1]).astype(BF16)

    neighbour_sums(0)
    if not LATE: fill(0)
    for q in range(1, chunks):
        line_arrivals(q)
        neighbour_sums(q)
        if not LATE: fill(q)
    for q in range(chunks if LATE else 0):
        fill(q)
    divide = value_columns[0]

    for q in range(chunks):
        mean_sum = total_out[q, c].astype(F32)
        for k in range(1, 4):
            arrived(total_copies[q][k - 1])
            mean_sum += total_in[q, k - 1].astype(F32)
        aggregate[:, cols(q)] = (mean_sum * divide).astype(BF16)
        if q < chunks - 1:
            value[...] += dot(aggregate[:, cols(q)], wneigh[cols(q), :])
    def exchange_aggregate():
        agg_t[...] = aggregate[...].astype(F32).T.astype(BF16).reshape(agg_t.shape)
        lhs[pl.ds(2, 2), :, here] = agg_t[:, me]
        slices.extend([
            send(agg_t.at[:, peer[1] * 2 + peer[2]], lhs.at[pl.ds(2, 2), :, here], peer)
            for peer in plane_all
        ])

    pg_copies, sib_pg = [], []
    for q in range(chunks):
        v = value[:, cols(q)] + dot(
            aggregate[:, cols(chunks - 1)], wneigh[cols(chunks - 1), cols(q)]
        )
        inner = jnp.tanh(ROOT * (v + 0.044715 * v * v * v))
        act_ref[:, cols(q)] = (0.5 * v * (1.0 + inner)).astype(BF16)
        slope = 0.5 * (1.0 + inner) + 0.5 * v * (1.0 - inner * inner) * (
            ROOT * (1.0 + 3.0 * 0.044715 * v * v)
        )
        pgs[q, p, c] = (cot[:, cols(q)].astype(F32) * slope).astype(BF16)
        if q >= ahead:
            for copy in pg_copies[q - ahead]:
                copy.wait_send()
                gone.add(id(copy))
        if SIBF: sib_pg.append([send(pgs.at[q, p, c], pgs.at[q, p, c], sibling)])
        pg_copies.append([send(pgs.at[q, p, c], pgs.at[q, p, c], peer) for peer in plane])
        if not SIBF: sib_pg.append([send(pgs.at[q, p, c], pgs.at[q, p, c], sibling)])
    total_self = dot(pgs[0, p, c], wself[:, cols(0)], ((1,), (1,)))
    for q in range(1, chunks):
        total_self += dot(pgs[q, p, c], wself[:, cols(q)], ((1,), (1,)))
    self_grad[...] = total_self

    if not MOVE: exchange_aggregate()
    gw_copies = []

    def weight_terms():
        for copy in slices:
            arrived(copy)
        for q in range(chunks):
            gw_out[:, :, cols(q)] = (
                dot(lhs[...].reshape(tile, wide), pgs[q].reshape(wide, part))
                .astype(BF16)
                .reshape(4, tile // 4, part)
            )

    def weight_sends():
        gw_copies.extend([
                send(gw_out.at[(r + k) % 4], gw_in.at[k - 1], line[k - 1]) for k in range(1, 4)
        ])

    relay, near_s, second_s, third_s, straight = [], [], [], [], []

    def follow(q):
        @pl.when(middle == 0)
        def _():
            third_s[q].start()
            near_s[q].start()

        @pl.when(middle == 1)
        def _():
            relay[q].wait_recv()
            joint = spread_out[q, place_of(3)].astype(F32) + spread_in[q, 3].astype(F32)
            spread_out[q, place_of(3)] = joint.astype(BF16)
            second_s[q][1].start()

    def plane_arrivals(q):
        for k in range(1, 4):
            arrived(pg_copies[q][k - 1])
            block = pgs.at[q, p, column(k)]
            sib_pg[q].append(send(block, block, sibling))

    for q in range(chunks if FWD else 0):
        plane_arrivals(q)
    for q in range(chunks):
        if not FWD: plane_arrivals(q)
        spread = dot(col_adj[0], pgs[q, p].reshape(half, part))
        for copy in sib_pg[q]:
            arrived(copy)
        spread += dot(col_adj[1], pgs[q, other].reshape(half, part))
        spread_out[q] = spread.astype(BF16).reshape(4, tile, part)
        if P4D:
            straight.append([
                send(spread_out.at[q, (r + k) % 4], spread_in.at[q, k - 1], line[k - 1])
                for k in (2, 1, 3)
            ])
        else:
            relay.append(copy_to(spread_out.at[q, place_of(3)], spread_in.at[q, 3], at_row(1)))
            third_s.append(copy_to(spread_out.at[q, place_of(2)], spread_in.at[q, 2], at_row(2)))
            near_s.append(
                copy_to(spread_out.at[q, place_of(1 - middle)], spread_in.at[q, 0], at_row(1 - middle))
            )
            second_s.append((
                copy_to(spread_out.at[q, place_of(2)], spread_in.at[q, 1], at_row(2)),
                copy_to(spread_out.at[q, place_of(3)], spread_in.at[q, 1], at_row(3)),
            ))

            @pl.when(middle == 0)
            def _():
                relay[q].start()

            @pl.when(middle == 1)
            def _():
                second_s[q][0].start()
                near_s[q].start()

            if q > 0:
                follow(q - 1)
    if GWE: weight_terms()
    if GWE == 2: weight_sends()
    if not P4D:
        follow(chunks - 1)
    if GWE == 0: weight_terms()
    if GWE < 2: weight_sends()

    total_self = self_grad[...]
    for q in range(chunks):
        if P4D:
            back = spread_out[q, r].astype(F32)
            for copy, k in zip(straight[q], (2, 1, 3)):
                copy.wait_recv()
                back += spread_in[q, k - 1].astype(F32)
            total_self += dot(back.astype(BF16), wneigh[:, cols(q)], ((1,), (1,)))
            continue
        near_s[q].wait_recv()
        value[:, cols(q)] = spread_out[q, r].astype(F32) + spread_in[q, 0].astype(F32)

        @pl.when(middle == 1)
        def _():
            second_s[q][0].wait_recv()
            third_s[q].wait_recv()
            value[:, cols(q)] += spread_in[q, 2].astype(F32)

        @pl.when(middle == 0)
        def _():
            second_s[q][1].wait_recv()

        back = (value[:, cols(q)] + spread_in[q, 1].astype(F32)).astype(BF16)
        total_self += dot(back, wneigh[:, cols(q)], ((1,), (1,)))
    gfeat_ref[...] = total_self.astype(BF16)
    grad = gw_out[r].astype(F32)
    for k in range(1, 4):
        gw_copies[k - 1].wait_recv()
        grad += gw_in[k - 1].astype(F32)
    gw_ref[...] = grad * (1.0 / math.sqrt(tile * 32))

    assert used[0] <= send_sem.shape[0]
    for copy in begun + near_s:
        if id(copy) not in gone:
            copy.wait_send()
    for q in range(max(chunks - ahead, 0), chunks):
        line_sent(q)

    @pl.when(middle == 1)
    def _():
        for q in range(chunks):
            for copy in (() if P1D else (onward[q],)) + (() if P4D else second_s[q]):
                copy.wait_send()

    @pl.when(middle == 0)
    def _():
        for copy in relay + third_s:
            copy.wait_send()


def finish_kernel(act_ref, gfeat_ref, gw_ref, act_out, gfeat_out, gw_out, sem):
    copies = [
        pltpu.make_async_copy(a, b, sem.at[i])
        for i, (a, b) in enumerate(((act_ref, act_out), (gfeat_ref, gfeat_out), (gw_ref, gw_out)))
    ]
    for copy in copies:
        copy.start()
    for copy in copies:
        copy.wait()


def fused_layer(features, w_self, w_neigh, cotangent, tile_row, tile_col, tile_mask, tile_count):
    tile, depth = features.shape
    slots = tile_mask.shape[0]
    q, part = CHUNKS, depth // CHUNKS
    piece = depth // 16
    wide = 8 * tile
    nsem = q * (5 + 4 + 3 + 3 + 4 + 5) + 5 + 7 + 14 + 3
    vmem = pl.BlockSpec(memory_space=pltpu.VMEM)
    results = pl.pallas_call(
        lambda *refs: layer_kernel(tile, depth, slots, q, AHEAD, *refs),
        out_shape=(
            pltpu.VMEM((tile, depth), BF16),
            pltpu.VMEM((tile, depth), BF16),
            pltpu.VMEM((piece, depth), F32),
        ),
        in_specs=[pl.BlockSpec(memory_space=pltpu.HBM)] * 8,
        out_specs=(vmem, vmem, vmem),
        scratch_shapes=[
            pltpu.VMEM((tile, depth), BF16),
            pltpu.VMEM((depth, depth), BF16),
            pltpu.VMEM((depth, depth), BF16),
            pltpu.VMEM((tile, depth), BF16),
            pltpu.VMEM((slots,), jnp.int32),
            pltpu.VMEM((slots,), jnp.int32),
            pltpu.SMEM((1,), jnp.int32),
            pltpu.VMEM((tile // 16, slots, 16, tile), jnp.int32),
            pltpu.VMEM((512, slots * 8), BF16),
            pltpu.VMEM((2, 2, 4, tile, 4 * tile), BF16),
            pltpu.VMEM((3, 4, tile, 4 * tile), BF16),
            pltpu.VMEM((2, 4 * tile, 4 * tile), BF16),
            pltpu.VMEM((2, 4 * tile, 4 * tile), BF16),
            pltpu.VMEM((q, 2, 4, tile, part), BF16),
            pltpu.VMEM((q, 4, tile, part), BF16),
            pltpu.VMEM((q, 3, tile, part), BF16),
            pltpu.VMEM((8, 8, tile), F32),
            pltpu.VMEM((8, tile), F32),
            pltpu.VMEM((2, 8, piece, tile), BF16),
            pltpu.VMEM((2, 8, piece, tile), BF16),
            pltpu.VMEM((4, piece, wide), BF16),
            pltpu.VMEM((q, 2, 4, tile, part), BF16),
            pltpu.VMEM((q, 4, tile, part), BF16),
            pltpu.VMEM((q, 4, tile, part), BF16),
            pltpu.VMEM((4, piece, depth), BF16),
            pltpu.VMEM((3, piece, depth), BF16),
            pltpu.VMEM((tile, depth), F32),
            pltpu.VMEM((tile, depth), BF16),
            pltpu.VMEM((tile, depth), F32),
            pltpu.SemaphoreType.DMA((7,)),
            pltpu.SemaphoreType.DMA((tile // 16,)),
            pltpu.SemaphoreType.DMA((nsem,)),
            pltpu.SemaphoreType.DMA((nsem,)),
        ],
        compiler_params=pltpu.CompilerParams(
            collective_id=0, has_side_effects=True, vmem_limit_bytes=LIMIT * 2**20
        ),
        name="layer",
    )(features, w_self, w_neigh, cotangent, tile_row, tile_col, tile_count, tile_mask)
    return pl.pallas_call(
        finish_kernel,
        out_shape=tuple(jax.ShapeDtypeStruct(x.shape, x.dtype) for x in results),
        in_specs=[vmem] * 3,
        out_specs=(pl.BlockSpec(memory_space=pl.ANY),) * 3,
        scratch_shapes=[pltpu.SemaphoreType.DMA((3,))],
        compiler_params=pltpu.CompilerParams(vmem_limit_bytes=2**20),
        name="finish",
    )(*results)


def shards(features, w_self, w_neigh, cotangent, tile_row, tile_col, tile_mask, tile_count):
    row_devices = lax.axis_size("row")
    col_devices = lax.axis_size("col")
    rep_devices = lax.axis_size("rep")
    device_total = row_devices * col_devices * rep_devices
    tile_size = features.shape[0]
    row_blocks = col_devices * rep_devices
    col_blocks = row_devices * rep_devices
    if (row_devices, col_devices, rep_devices) == (4, 4, 2):
        return fused_layer(
            features, w_self, w_neigh, cotangent, tile_row, tile_col, tile_mask, tile_count
        )
    adjacency = build_adjacency(tile_row, tile_col, tile_count, tile_mask, row_blocks, col_blocks)
    gathered = lax.all_gather(features, ("row", "rep"), axis=0, tiled=True)
    totals = jnp.dot(adjacency, gathered, preferred_element_type=jnp.float32)
    degree = jnp.sum(adjacency.astype(jnp.float32), axis=1)
    own_sum, own_degree = (
        lax.psum_scatter(totals, ("col", "rep"), scatter_dimension=0, tiled=True),
        lax.psum_scatter(degree, ("col", "rep"), scatter_dimension=0, tiled=True),
    )
    divisor = own_degree[:, None] + 1.0
    aggregate = (own_sum / divisor).astype(jnp.bfloat16)
    preact = jnp.dot(features, w_self, preferred_element_type=jnp.float32) + jnp.dot(
        aggregate, w_neigh, preferred_element_type=jnp.float32
    )
    activated, pullback = jax.vjp(lambda value: jax.nn.gelu(value, approximate=True), preact)
    pre_grad = pullback(cotangent.astype(jnp.float32))[0].astype(jnp.bfloat16)
    inv_root = 1.0 / math.sqrt(tile_size * device_total)
    local_grads = (
        jnp.concatenate(
            [
                jnp.dot(features.T, pre_grad, preferred_element_type=jnp.float32),
                jnp.dot(aggregate.T, pre_grad, preferred_element_type=jnp.float32),
            ],
            axis=0,
        )
        * inv_root
    )
    neighbour_grad = (
        jnp.dot(pre_grad, w_neigh.T, preferred_element_type=jnp.float32) / divisor
    ).astype(jnp.bfloat16)
    slab_grads = lax.all_gather(neighbour_grad, ("col", "rep"), axis=0, tiled=True)
    grad_weights = lax.psum_scatter(
        local_grads, ("row", "col", "rep"), scatter_dimension=0, tiled=True
    )
    spread = lax.dot_general(
        adjacency, slab_grads, (((0,), (0,)), ((), ())), preferred_element_type=jnp.float32
    )
    returned = lax.psum_scatter(spread, ("row", "rep"), scatter_dimension=0, tiled=True)
    grad_features = (
        jnp.dot(pre_grad, w_self.T, preferred_element_type=jnp.float32) + returned
    ).astype(jnp.bfloat16)
    return (activated.astype(jnp.bfloat16), grad_features, grad_weights)


def solution(mesh):
    placed = (
        P(("row", "col", "rep"), None),
        P(),
        P(),
        P(("row", "col", "rep"), None),
        P(("row", "col", "rep")),
        P(("row", "col", "rep")),
        P(("row", "col", "rep"), None, None),
        P(("row", "col", "rep")),
    )
    return jax.shard_map(
        shards,
        mesh=mesh,
        in_specs=placed,
        out_specs=(
            P(("row", "col", "rep"), None),
            P(("row", "col", "rep"), None),
            P(("row", "col", "rep"), None),
        ),
        check_vma=False,
    )
```

```python
import math

import jax
import jax.numpy as jnp
from jax import lax
from jax.experimental import pallas as pl
from jax.experimental.pallas import tpu as pltpu
from jax.sharding import PartitionSpec as P

MESH_ID = pl.DeviceIdType.MESH
F32 = jnp.float32
BF16 = jnp.bfloat16
ROOT = math.sqrt(2.0 / math.pi)


def build_kernel(group, tile, rows_ref, cols_ref, count_ref, mask_ref, adj_ref):
    step = pl.program_id(0)

    @pl.when(step == 0)
    def _():
        adj_ref[...] = jnp.zeros_like(adj_ref)

    for lane in range(group):
        slot = step * group + lane

        @pl.when(slot < count_ref[0])
        def _():
            row = pl.multiple_of(rows_ref[slot] * tile, tile)
            col = pl.multiple_of(cols_ref[slot] * tile, tile)
            where = (pl.ds(row, tile), pl.ds(col, tile))
            adj_ref[where] += mask_ref[lane].astype(jnp.float32).astype(jnp.bfloat16)


def build_adjacency(tile_row, tile_col, tile_count, tile_mask, row_blocks, col_blocks):
    slots, tile, _ = tile_mask.shape
    group = math.gcd(slots, 8)
    shape = (row_blocks * tile, col_blocks * tile)
    return pl.pallas_call(
        lambda *refs: build_kernel(group, tile, *refs),
        out_shape=jax.ShapeDtypeStruct(shape, jnp.bfloat16),
        grid_spec=pltpu.PrefetchScalarGridSpec(
            num_scalar_prefetch=3,
            grid=(slots // group,),
            in_specs=[pl.BlockSpec((group, tile, tile), lambda step, *_: (step, 0, 0))],
            out_specs=pl.BlockSpec(shape, lambda step, *_: (0, 0)),
        ),
        compiler_params=pltpu.CompilerParams(vmem_limit_bytes=48 * 2**20),
        cost_estimate=pl.CostEstimate(
            flops=slots * tile * tile, bytes_accessed=slots * tile * tile * 4, transcendentals=0
        ),
    )(tile_row, tile_col, tile_count, tile_mask)


def dot(a, b, dims=((1,), (0,))):
    return lax.dot_general(a, b, (dims, ((), ())), preferred_element_type=F32)


CHUNKS = 2
MOVE = 0
GWE = 1
DG2 = 1
DG3 = 1
FWD = 0
SIBF = 1
LIMIT = 56
AHEAD = 2
P1D = 0
P4D = 0
LATE = 1


def layer_kernel(
    tile, depth, slots, chunks, ahead,
    feat_ref, wself_ref, wneigh_ref, cot_ref, trow_ref, tcol_ref, count_ref, mask_ref,
    act_ref, gfeat_ref, gw_ref,
    feat, wself, wneigh, cot, trow, tcol, count, mask, place,
    own_adj, adj_in, row_adj, col_adj, nodes, total_out, total_in,
    deg_in, rdeg, feat_t, agg_t, lhs, pgs, spread_out, spread_in, gw_out, gw_in,
    value, aggregate, self_grad,
    local_sem, mask_sem, send_sem, recv_sem,
):
    r, c, p = lax.axis_index("row"), lax.axis_index("col"), lax.axis_index("rep")
    other = 1 - p
    me = c * 2 + p
    order = p * 4 + c
    wide, half = 8 * tile, 4 * tile
    part = depth // chunks

    def cols(q):
        return pl.ds(q * part, part)

    low = 1 - r // 2
    middle = r * low + (3 - r) * (1 - low)

    def place_of(v):
        return low * v + (1 - low) * (3 - v)

    def at_row(v):
        return (place_of(v), c, p)

    def column(k):
        return (c // 2 + k // 2) % 2 * 2 + (c % 2 + k % 2) % 2

    used = [0]
    begun = []
    gone = set()

    def copy_to(src, dst, device):
        at = used[0]
        used[0] += 1
        return pltpu.make_async_remote_copy(
            src_ref=src, dst_ref=dst, send_sem=send_sem.at[at], recv_sem=recv_sem.at[at],
            device_id=device, device_id_type=MESH_ID,
        )

    def send(src, dst, device):
        copy = copy_to(src, dst, device)
        copy.start()
        begun.append(copy)
        return copy


    def arrived(copy):
        copy.wait_recv()

    sibling = (r, c, other)
    line = [((r + k) % 4, c, p) for k in range(1, 4)]
    plane = [(r, column(k), p) for k in range(1, 4)]
    plane_all = plane + [(r, column(k), other) for k in range(4)]

    barrier = pltpu.get_barrier_semaphore()
    for peer in line + plane_all:
        pl.semaphore_signal(barrier, inc=1, device_id=peer, device_id_type=MESH_ID)

    loads = [
        pltpu.make_async_copy(a, b, local_sem.at[i])
        for i, (a, b) in enumerate((
            (trow_ref, trow), (tcol_ref, tcol), (count_ref, count), (feat_ref, feat),
            (wself_ref, wself), (wneigh_ref, wneigh), (cot_ref, cot),
        ))
    ]
    for load in loads[:3]:
        load.start()
    groups = [
        pltpu.make_async_copy(mask_ref.at[:, pl.ds(g * 16, 16), :], mask.at[g], mask_sem.at[g])
        for g in range(tile // 16)
    ]
    for load in loads[3:4]:
        load.start()
    for group in groups:
        group.start()
    for load in loads[4:]:
        load.start()

    pl.semaphore_wait(barrier, 10)

    near, across, inward, outward, onward, sib_feat = [], [], [], [], [], []
    direct = []
    for q in range(chunks if P1D else 0):
        src, dst = feat_ref.at[:, cols(q)], nodes.at[q, p, r]
        base = used[0]
        direct.append((base, [copy_to(src, dst, peer) for peer in line]))
    for q in range(0 if P1D else chunks):
        src, dst = feat_ref.at[:, cols(q)], nodes.at[q, p, r]
        far = nodes.at[q, p, place_of(3)]
        near.append(copy_to(src, dst, at_row(1 - middle)))
        across.append(copy_to(src, dst, at_row(2)))
        inward.append(copy_to(src, dst, at_row(2)))
        outward.append(copy_to(src, dst, at_row(3)))
        onward.append(copy_to(far, far, at_row(0)))

    def line_start(q):
        if P1D:
            for k in (1, 0, 2):
                direct[q][1][k].start()
            return

        @pl.when(middle == 0)
        def _():
            inward[q].start()

        @pl.when(middle == 1)
        def _():
            outward[q].start()
            across[q].start()

        near[q].start()

    def line_sent(q):
        if P1D:
            for copy in direct[q][1]:
                copy.wait_send()
            return

        near[q].wait_send()

        @pl.when(middle == 0)
        def _():
            inward[q].wait_send()

        @pl.when(middle == 1)
        def _():
            outward[q].wait_send()
            across[q].wait_send()

    if SIBF:
        for q in range(chunks):
            sib_feat.append([send(feat_ref.at[:, cols(q)], nodes.at[q, p, r], sibling)])
    for q in range(min(ahead, chunks)):
        line_start(q)
    for q in range(0 if SIBF else chunks):
        sib_feat.append([send(feat_ref.at[:, cols(q)], nodes.at[q, p, r], sibling)])
    for load in loads[:3]:
        load.wait()
    lane = lax.broadcasted_iota(jnp.int32, (8, slots), 1)
    cell = jnp.broadcast_to((trow[...] * 8 + tcol[...]).reshape(1, slots), (8, slots))
    cell = jnp.where(lane < count[0], cell, 64).astype(F32).astype(BF16)
    gap = lax.broadcasted_iota(jnp.int32, (slots, slots * 8), 1) - 8 * lax.broadcasted_iota(
        jnp.int32, (slots, slots * 8), 0
    )
    repeat = jnp.where((gap >= 0) & (gap < 8), 1.0, 0.0).astype(BF16)
    key = dot(cell, repeat)[0:1] * 8.0 + (
        lax.broadcasted_iota(jnp.int32, (1, slots * 8), 1) % 8
    ).astype(F32)
    spot = lax.broadcasted_iota(jnp.int32, (512, slots * 8), 0).astype(F32)
    place[...] = jnp.where(spot == key, 1.0, 0.0).astype(BF16)

    loads[3].wait()
    here = pl.ds(pl.multiple_of(order * tile, tile), tile)
    feat_t[...] = feat[...].astype(F32).T.astype(BF16).reshape(feat_t.shape)
    lhs[pl.ds(0, 2), :, here] = feat_t[:, me]
    for q in range(chunks):
        nodes[q, p, r] = feat[:, q * part : (q + 1) * part]
    slices = [
        send(feat_t.at[:, peer[1] * 2 + peer[2]], lhs.at[pl.ds(0, 2), :, here], peer)
        for peer in plane_all
    ]

    def build(g, carry):
        pltpu.make_async_copy(
            mask_ref.at[:, pl.ds(g * 16, 16), :], mask.at[g], mask_sem.at[g]
        ).wait()
        x = jnp.concatenate(
            [
                mask[g, :, 0:8, :].reshape(slots * 8, tile).astype(F32).astype(BF16),
                mask[g, :, 8:16, :].reshape(slots * 8, tile).astype(F32).astype(BF16),
            ],
            axis=1,
        )
        res = dot(place[...], x)
        for i in range(8):
            for j in range(8):
                at = (i * 8 + j) * 8
                both = jnp.concatenate([res[at : at + 8, :tile], res[at : at + 8, tile:]], axis=0)
                own_adj[j % 2, i % 2, i // 2, pl.ds(pl.multiple_of(g * 16, 16), 16),
                        j // 2 * tile : (j // 2 + 1) * tile] = both.astype(BF16)
        return carry

    lax.fori_loop(0, tile // 16, build, 0)

    @pl.when(middle == 1)
    def _():
        for q in range(chunks):
            inward[q].wait_recv()
            onward[q].start()

    for q in range(ahead, chunks):
        line_sent(q - ahead)
        line_start(q)

    adj_copies = [
        send(own_adj.at[b, a], adj_in.at[i], sibling)
        for i, (b, a) in enumerate(((other, other), (p, other), (other, p)))
    ]

    def line_arrivals(q):
        def onto(k):
            block = nodes.at[q, p, place_of(k)]
            sib_feat[q].append(send(block, block, sibling))

        if P1D:
            for v in (1 - middle, 2, 3):
                source = place_of(v)
                at = direct[q][0] + (r + 3 - source) % 4
                block = nodes.at[q, p, source]
                pltpu.make_async_remote_copy(
                    src_ref=block, dst_ref=block, send_sem=send_sem.at[at],
                    recv_sem=recv_sem.at[at], device_id=sibling, device_id_type=MESH_ID,
                ).wait_recv()
                onto(v)
            return

        near[q].wait_recv()
        onto(1 - middle)

        @pl.when(middle == 1)
        def _():
            across[q].wait_recv()

        @pl.when(middle == 0)
        def _():
            outward[q].wait_recv()

        onto(2)

        @pl.when(middle == 0)
        def _():
            onward[q].wait_recv()

        onto(3)

    for load in loads[4:]:
        load.wait()

    ones = jnp.ones((8, half), BF16)
    sums = dot(ones, own_adj[0].reshape(wide, half), ((1,), (1,)))
    sums += dot(ones, own_adj[1].reshape(wide, half), ((1,), (1,)))
    which = lax.broadcasted_iota(jnp.int32, (8, tile), 0)
    packed = jnp.zeros((8, tile), F32)
    for k in range(8):
        packed += jnp.where(which == k, sums[:, k * tile : (k + 1) * tile], 0.0)
    deg_in[0] = packed
    deg_copies = [send(deg_in.at[0], deg_in.at[k + 1], peer) for k, peer in enumerate(plane_all)]

    line_arrivals(0)
    arrived(adj_copies[0])
    row_adj[0] = (own_adj[p, p] + adj_in[0]).reshape(half, half)
    arrived(adj_copies[1])
    row_adj[1] = (own_adj[other, p] + adj_in[1]).reshape(half, half)

    total_copies = []

    def neighbour_sums(q):
        total = dot(row_adj[0], nodes[q, p].reshape(half, part))
        for copy in sib_feat[q]:
            arrived(copy)
        total += dot(row_adj[1], nodes[q, other].reshape(half, part))
        total_out[q] = total.astype(BF16).reshape(4, tile, part)
        begun_here = {
            k: send(total_out.at[q, column(k)], total_in.at[q, k - 1], plane[k - 1])
            for k in ((3, 1, 2) if DG2 else (1, 2, 3))
        }
        total_copies.append([begun_here[k] for k in range(1, 4)])

    value_columns = []

    def fill(q):
        if q == 0:
            value[...] = dot(feat[...], wself[...])
            for copy in deg_copies:
                arrived(copy)
            degree = deg_in[0]
            for k in range(1, 8):
                degree += deg_in[k]
            rdeg[...] = 1.0 / (degree + 1.0)
        if q == min(1, chunks - 1):
            value_columns.append(jnp.broadcast_to(rdeg[pl.ds(order, 1), :], (8, tile)).T[:, 0:1])
            scales = [
                jnp.concatenate([rdeg[pl.ds(rep * 4 + k, 1), :] for k in range(4)], axis=1)
                for rep in (p, other)
            ]
            col_adj[0] = (row_adj[0].astype(F32).T * scales[0]).astype(BF16)
            arrived(adj_copies[2])
            both = (own_adj[p, other] + adj_in[2]).reshape(half, half).astype(F32)
            col_adj[1] = (both.T * scales[1]).astype(BF16)

    neighbour_sums(0)
    if not LATE: fill(0)
    for q in range(1, chunks):
        line_arrivals(q)
        neighbour_sums(q)
        if not LATE: fill(q)
    for q in range(chunks if LATE else 0):
        fill(q)
    divide = value_columns[0]

    for q in range(chunks):
        mean_sum = total_out[q, c].astype(F32)
        for k in range(1, 4):
            arrived(total_copies[q][k - 1])
            mean_sum += total_in[q, k - 1].astype(F32)
        aggregate[:, cols(q)] = (mean_sum * divide).astype(BF16)
        if q < chunks - 1:
            value[...] += dot(aggregate[:, cols(q)], wneigh[cols(q), :])
    def exchange_aggregate():
        agg_t[...] = aggregate[...].astype(F32).T.astype(BF16).reshape(agg_t.shape)
        lhs[pl.ds(2, 2), :, here] = agg_t[:, me]
        slices.extend([
            send(agg_t.at[:, peer[1] * 2 + peer[2]], lhs.at[pl.ds(2, 2), :, here], peer)
            for peer in plane_all
        ])

    pg_copies, sib_pg = [], []
    for q in range(chunks):
        v = value[:, cols(q)] + dot(
            aggregate[:, cols(chunks - 1)], wneigh[cols(chunks - 1), cols(q)]
        )
        inner = jnp.tanh(ROOT * (v + 0.044715 * v * v * v))
        act_ref[:, cols(q)] = (0.5 * v * (1.0 + inner)).astype(BF16)
        slope = 0.5 * (1.0 + inner) + 0.5 * v * (1.0 - inner * inner) * (
            ROOT * (1.0 + 3.0 * 0.044715 * v * v)
        )
        pgs[q, p, c] = (cot[:, cols(q)].astype(F32) * slope).astype(BF16)
        if q >= ahead:
            for copy in pg_copies[q - ahead]:
                copy.wait_send()
                gone.add(id(copy))
        if SIBF: sib_pg.append([send(pgs.at[q, p, c], pgs.at[q, p, c], sibling)])
        begun_here = {
            k: send(pgs.at[q, p, c], pgs.at[q, p, c], plane[k - 1])
            for k in ((3, 1, 2) if DG3 else (1, 2, 3))
        }
        pg_copies.append([begun_here[k] for k in range(1, 4)])
        if not SIBF: sib_pg.append([send(pgs.at[q, p, c], pgs.at[q, p, c], sibling)])
    total_self = dot(pgs[0, p, c], wself[:, cols(0)], ((1,), (1,)))
    for q in range(1, chunks):
        total_self += dot(pgs[q, p, c], wself[:, cols(q)], ((1,), (1,)))
    self_grad[...] = total_self

    if not MOVE: exchange_aggregate()
    gw_copies = []

    def weight_terms():
        for copy in slices:
            arrived(copy)
        for q in range(chunks):
            gw_out[:, :, cols(q)] = (
                dot(lhs[...].reshape(tile, wide), pgs[q].reshape(wide, part))
                .astype(BF16)
                .reshape(4, tile // 4, part)
            )

    def weight_sends():
        gw_copies.extend([
                send(gw_out.at[(r + k) % 4], gw_in.at[k - 1], line[k - 1]) for k in range(1, 4)
        ])

    relay, near_s, second_s, third_s, straight = [], [], [], [], []

    def follow(q):
        @pl.when(middle == 0)
        def _():
            third_s[q].start()
            near_s[q].start()

        @pl.when(middle == 1)
        def _():
            relay[q].wait_recv()
            joint = spread_out[q, place_of(3)].astype(F32) + spread_in[q, 3].astype(F32)
            spread_out[q, place_of(3)] = joint.astype(BF16)
            second_s[q][1].start()

    def plane_arrivals(q):
        for k in range(1, 4):
            arrived(pg_copies[q][k - 1])
            block = pgs.at[q, p, column(k)]
            sib_pg[q].append(send(block, block, sibling))

    for q in range(chunks if FWD else 0):
        plane_arrivals(q)
    for q in range(chunks):
        if not FWD: plane_arrivals(q)
        spread = dot(col_adj[0], pgs[q, p].reshape(half, part))
        for copy in sib_pg[q]:
            arrived(copy)
        spread += dot(col_adj[1], pgs[q, other].reshape(half, part))
        spread_out[q] = spread.astype(BF16).reshape(4, tile, part)
        if P4D:
            straight.append([
                send(spread_out.at[q, (r + k) % 4], spread_in.at[q, k - 1], line[k - 1])
                for k in (2, 1, 3)
            ])
        else:
            relay.append(copy_to(spread_out.at[q, place_of(3)], spread_in.at[q, 3], at_row(1)))
            third_s.append(copy_to(spread_out.at[q, place_of(2)], spread_in.at[q, 2], at_row(2)))
            near_s.append(
                copy_to(spread_out.at[q, place_of(1 - middle)], spread_in.at[q, 0], at_row(1 - middle))
            )
            second_s.append((
                copy_to(spread_out.at[q, place_of(2)], spread_in.at[q, 1], at_row(2)),
                copy_to(spread_out.at[q, place_of(3)], spread_in.at[q, 1], at_row(3)),
            ))

            @pl.when(middle == 0)
            def _():
                relay[q].start()

            @pl.when(middle == 1)
            def _():
                second_s[q][0].start()
                near_s[q].start()

            if q > 0:
                follow(q - 1)
    if GWE: weight_terms()
    if GWE == 2: weight_sends()
    if not P4D:
        follow(chunks - 1)
    if GWE == 0: weight_terms()
    if GWE < 2: weight_sends()

    total_self = self_grad[...]
    for q in range(chunks):
        if P4D:
            back = spread_out[q, r].astype(F32)
            for copy, k in zip(straight[q], (2, 1, 3)):
                copy.wait_recv()
                back += spread_in[q, k - 1].astype(F32)
            total_self += dot(back.astype(BF16), wneigh[:, cols(q)], ((1,), (1,)))
            continue
        near_s[q].wait_recv()
        value[:, cols(q)] = spread_out[q, r].astype(F32) + spread_in[q, 0].astype(F32)

        @pl.when(middle == 1)
        def _():
            second_s[q][0].wait_recv()
            third_s[q].wait_recv()
            value[:, cols(q)] += spread_in[q, 2].astype(F32)

        @pl.when(middle == 0)
        def _():
            second_s[q][1].wait_recv()

        back = (value[:, cols(q)] + spread_in[q, 1].astype(F32)).astype(BF16)
        total_self += dot(back, wneigh[:, cols(q)], ((1,), (1,)))
    gfeat_ref[...] = total_self.astype(BF16)
    grad = gw_out[r].astype(F32)
    for k in range(1, 4):
        gw_copies[k - 1].wait_recv()
        grad += gw_in[k - 1].astype(F32)
    gw_ref[...] = grad * (1.0 / math.sqrt(tile * 32))

    assert used[0] <= send_sem.shape[0]
    for copy in begun + near_s:
        if id(copy) not in gone:
            copy.wait_send()
    for q in range(max(chunks - ahead, 0), chunks):
        line_sent(q)

    @pl.when(middle == 1)
    def _():
        for q in range(chunks):
            for copy in (() if P1D else (onward[q],)) + (() if P4D else second_s[q]):
                copy.wait_send()

    @pl.when(middle == 0)
    def _():
        for copy in relay + third_s:
            copy.wait_send()


def finish_kernel(act_ref, gfeat_ref, gw_ref, act_out, gfeat_out, gw_out, sem):
    copies = [
        pltpu.make_async_copy(a, b, sem.at[i])
        for i, (a, b) in enumerate(((act_ref, act_out), (gfeat_ref, gfeat_out), (gw_ref, gw_out)))
    ]
    for copy in copies:
        copy.start()
    for copy in copies:
        copy.wait()


def fused_layer(features, w_self, w_neigh, cotangent, tile_row, tile_col, tile_mask, tile_count):
    tile, depth = features.shape
    slots = tile_mask.shape[0]
    q, part = CHUNKS, depth // CHUNKS
    piece = depth // 16
    wide = 8 * tile
    nsem = q * (5 + 4 + 3 + 3 + 4 + 5) + 5 + 7 + 14 + 3
    vmem = pl.BlockSpec(memory_space=pltpu.VMEM)
    results = pl.pallas_call(
        lambda *refs: layer_kernel(tile, depth, slots, q, AHEAD, *refs),
        out_shape=(
            pltpu.VMEM((tile, depth), BF16),
            pltpu.VMEM((tile, depth), BF16),
            pltpu.VMEM((piece, depth), F32),
        ),
        in_specs=[pl.BlockSpec(memory_space=pltpu.HBM)] * 8,
        out_specs=(vmem, vmem, vmem),
        scratch_shapes=[
            pltpu.VMEM((tile, depth), BF16),
            pltpu.VMEM((depth, depth), BF16),
            pltpu.VMEM((depth, depth), BF16),
            pltpu.VMEM((tile, depth), BF16),
            pltpu.VMEM((slots,), jnp.int32),
            pltpu.VMEM((slots,), jnp.int32),
            pltpu.SMEM((1,), jnp.int32),
            pltpu.VMEM((tile // 16, slots, 16, tile), jnp.int32),
            pltpu.VMEM((512, slots * 8), BF16),
            pltpu.VMEM((2, 2, 4, tile, 4 * tile), BF16),
            pltpu.VMEM((3, 4, tile, 4 * tile), BF16),
            pltpu.VMEM((2, 4 * tile, 4 * tile), BF16),
            pltpu.VMEM((2, 4 * tile, 4 * tile), BF16),
            pltpu.VMEM((q, 2, 4, tile, part), BF16),
            pltpu.VMEM((q, 4, tile, part), BF16),
            pltpu.VMEM((q, 3, tile, part), BF16),
            pltpu.VMEM((8, 8, tile), F32),
            pltpu.VMEM((8, tile), F32),
            pltpu.VMEM((2, 8, piece, tile), BF16),
            pltpu.VMEM((2, 8, piece, tile), BF16),
            pltpu.VMEM((4, piece, wide), BF16),
            pltpu.VMEM((q, 2, 4, tile, part), BF16),
            pltpu.VMEM((q, 4, tile, part), BF16),
            pltpu.VMEM((q, 4, tile, part), BF16),
            pltpu.VMEM((4, piece, depth), BF16),
            pltpu.VMEM((3, piece, depth), BF16),
            pltpu.VMEM((tile, depth), F32),
            pltpu.VMEM((tile, depth), BF16),
            pltpu.VMEM((tile, depth), F32),
            pltpu.SemaphoreType.DMA((7,)),
            pltpu.SemaphoreType.DMA((tile // 16,)),
            pltpu.SemaphoreType.DMA((nsem,)),
            pltpu.SemaphoreType.DMA((nsem,)),
        ],
        compiler_params=pltpu.CompilerParams(
            collective_id=0, has_side_effects=True, vmem_limit_bytes=LIMIT * 2**20
        ),
        name="layer",
    )(features, w_self, w_neigh, cotangent, tile_row, tile_col, tile_count, tile_mask)
    return pl.pallas_call(
        finish_kernel,
        out_shape=tuple(jax.ShapeDtypeStruct(x.shape, x.dtype) for x in results),
        in_specs=[vmem] * 3,
        out_specs=(pl.BlockSpec(memory_space=pl.ANY),) * 3,
        scratch_shapes=[pltpu.SemaphoreType.DMA((3,))],
        compiler_params=pltpu.CompilerParams(vmem_limit_bytes=2**20),
        name="finish",
    )(*results)


def shards(features, w_self, w_neigh, cotangent, tile_row, tile_col, tile_mask, tile_count):
    row_devices = lax.axis_size("row")
    col_devices = lax.axis_size("col")
    rep_devices = lax.axis_size("rep")
    device_total = row_devices * col_devices * rep_devices
    tile_size = features.shape[0]
    row_blocks = col_devices * rep_devices
    col_blocks = row_devices * rep_devices
    if (row_devices, col_devices, rep_devices) == (4, 4, 2):
        return fused_layer(
            features, w_self, w_neigh, cotangent, tile_row, tile_col, tile_mask, tile_count
        )
    adjacency = build_adjacency(tile_row, tile_col, tile_count, tile_mask, row_blocks, col_blocks)
    gathered = lax.all_gather(features, ("row", "rep"), axis=0, tiled=True)
    totals = jnp.dot(adjacency, gathered, preferred_element_type=jnp.float32)
    degree = jnp.sum(adjacency.astype(jnp.float32), axis=1)
    own_sum, own_degree = (
        lax.psum_scatter(totals, ("col", "rep"), scatter_dimension=0, tiled=True),
        lax.psum_scatter(degree, ("col", "rep"), scatter_dimension=0, tiled=True),
    )
    divisor = own_degree[:, None] + 1.0
    aggregate = (own_sum / divisor).astype(jnp.bfloat16)
    preact = jnp.dot(features, w_self, preferred_element_type=jnp.float32) + jnp.dot(
        aggregate, w_neigh, preferred_element_type=jnp.float32
    )
    activated, pullback = jax.vjp(lambda value: jax.nn.gelu(value, approximate=True), preact)
    pre_grad = pullback(cotangent.astype(jnp.float32))[0].astype(jnp.bfloat16)
    inv_root = 1.0 / math.sqrt(tile_size * device_total)
    local_grads = (
        jnp.concatenate(
            [
                jnp.dot(features.T, pre_grad, preferred_element_type=jnp.float32),
                jnp.dot(aggregate.T, pre_grad, preferred_element_type=jnp.float32),
            ],
            axis=0,
        )
        * inv_root
    )
    neighbour_grad = (
        jnp.dot(pre_grad, w_neigh.T, preferred_element_type=jnp.float32) / divisor
    ).astype(jnp.bfloat16)
    slab_grads = lax.all_gather(neighbour_grad, ("col", "rep"), axis=0, tiled=True)
    grad_weights = lax.psum_scatter(
        local_grads, ("row", "col", "rep"), scatter_dimension=0, tiled=True
    )
    spread = lax.dot_general(
        adjacency, slab_grads, (((0,), (0,)), ((), ())), preferred_element_type=jnp.float32
    )
    returned = lax.psum_scatter(spread, ("row", "rep"), scatter_dimension=0, tiled=True)
    grad_features = (
        jnp.dot(pre_grad, w_self.T, preferred_element_type=jnp.float32) + returned
    ).astype(jnp.bfloat16)
    return (activated.astype(jnp.bfloat16), grad_features, grad_weights)


def solution(mesh):
    placed = (
        P(("row", "col", "rep"), None),
        P(),
        P(),
        P(("row", "col", "rep"), None),
        P(("row", "col", "rep")),
        P(("row", "col", "rep")),
        P(("row", "col", "rep"), None, None),
        P(("row", "col", "rep")),
    )
    return jax.shard_map(
        shards,
        mesh=mesh,
        in_specs=placed,
        out_specs=(
            P(("row", "col", "rep"), None),
            P(("row", "col", "rep"), None),
            P(("row", "col", "rep"), None),
        ),
        check_vma=False,
    )
```
